512 devices in a mesh: req: 64 (over x, z, core), tp: 8 (over y).
Axes of the slice: x: 4, y: 8, z: 8, core: 2. Of those that a mesh axis runs over, the one named last changes fastest.
Arguments:
- queries: bfloat16 [4, 512, 1024], P(None, 'req', 'tp'), may hold values from -6 to 6
- new_kv: bfloat16 [4, 512, 2, 1024], P(None, 'req', None, 'tp'), may hold values from -4 to 4
- residual: bfloat16 [4, 512, 2048], P(None, 'req'), may hold values from -1.1953125 to 1.1953125
- home_cache: bfloat16 [256, 128, 2, 1024], P('req', None, None, 'tp'), may hold values from -6 to 6
- prompt_cache: bfloat16 [256, 128, 2, 1024], P('req', None, None, 'tp'), may hold values from -6 to 6
- home_table: int32 [512, 4], P('req'), may hold values from 0 to 3
- home_len: int32 [512], P('req'), may hold values from 1 to 512, as said below
- parents: int32 [4, 512], P(None, 'req'), may hold values from 0 to 7
- prompt_place: int32 [64], P('req'), may hold values from 0 to 63, as said below
- owned_request: int32 [64], P('req'), may hold values from 0 to 63, as said below
- prompt_len: int32 [64], P('req'), may hold values from 1 to 512, as said below
- out_weight: bfloat16 [1024, 2048], P('tp'), may hold values from -0.1875 to 0.1875
- norm_gain: bfloat16 [2048], replicated, may hold values from 0.099609375 to 1.8984375
- qkv_weight: bfloat16 [2048, 3, 1024], P(None, None, 'tp'), may hold values from -0.03125 to 0.03125
Outputs:
- next_qkv: bfloat16 [4, 512, 3, 1024], P(None, 'req', None, 'tp')
- new_residual: bfloat16 [4, 512, 2048], P(None, 'req')
The draws below stay inside these ranges and needn't reach their ends.
Inputs may be any that keep to these rules, and one draw needn't show every extreme that they name: `home_len`: some beam has all 512 tokens. `prompt_len`: some prompt has all 512 tokens. `prompt_place`: A permutation. Slot j lies on device j. The 1 request of one device have their prompts on 1 different devices, each device holds prompts of 1 request of different devices, and a request's position among its device's requests equals its slot's position j % 1. `owned_request`: the inverse permutation of prompt_place.
All inputs are finite; a program needn't handle non-finite values.
Results may differ from the reference program's by a relative error of at most 0.013.
Values may be sent and summed in bfloat16 or wider, within the bound.
No kernel may reach another device: no remote copies, remote signals or barrier semaphores. Data moves between devices by JAX's collectives and lax.ppermute only.
A program may use at most 64 MiB of HBM per device.

```python
import math
import jax
import jax.numpy as jnp
from jax import lax

D = 2048
HEADS = 16
HEAD_DIM = 64
BLOCK = 128
BEAMS = 8
HOME_BLOCKS = 4
PROMPT_BLOCKS = 4
STEPS = 4
REQ_DEV = 1
REQUESTS = 64
BEAMS_DEV = 8
ROWS = 512
POOL_DEV = 4


def cache_blocks(key, salt, block_total):
    first, second = jax.random.split(jax.random.fold_in(key, salt))
    array_shape = (block_total, BLOCK, HEADS * HEAD_DIM)
    key_part = jnp.clip(jax.random.normal(first, array_shape, jnp.float32), -4.0, 4.0)
    value_part = jnp.clip(jax.random.normal(second, array_shape, jnp.float32), -4.0, 4.0)
    return jnp.stack([key_part, value_part], axis=2).astype(jnp.bfloat16)


def draw_home_cache(key, part):
    return cache_blocks(key, 1, POOL_DEV * REQUESTS // REQ_DEV)


def draw_prompt_cache(key, part):
    return cache_blocks(key, 2, PROMPT_BLOCKS * REQUESTS)


def draw_queries(key, part):
    array_shape = (STEPS, BEAMS * REQUESTS, HEADS * HEAD_DIM)
    first = jax.random.fold_in(key, 3)
    result = jnp.clip(jax.random.normal(first, array_shape, jnp.float32), -4.0, 4.0)
    return result.astype(jnp.bfloat16)


def draw_home_len(key, part):
    most_tokens = HOME_BLOCKS * BLOCK
    drawn = jax.random.randint(jax.random.fold_in(key, 5), (BEAMS * REQUESTS,), 1, most_tokens + 1)
    return drawn.at[0].set(most_tokens).astype(jnp.int32)


def draw_prompt_len(key, part):
    most_tokens = PROMPT_BLOCKS * BLOCK
    drawn = jax.random.randint(jax.random.fold_in(key, 6), (REQUESTS,), 1, most_tokens + 1)
    return drawn.at[REQUESTS - 1].set(most_tokens).astype(jnp.int32)


def placement(key):
    device_total = REQUESTS // REQ_DEV
    salted = jax.random.fold_in(key, 4242)
    owner_perm = jax.random.permutation(jax.random.fold_in(salted, 1), device_total)
    home_perm = jax.random.permutation(jax.random.fold_in(salted, 2), device_total)
    offsets = jax.random.permutation(jax.random.fold_in(salted, 3), device_total)[:REQ_DEV]
    request_ids = jnp.arange(REQUESTS, dtype=jnp.int32)
    home_device = request_ids // REQ_DEV
    local_index = request_ids % REQ_DEV
    owner_slot = owner_perm[(home_perm[home_device] + offsets[local_index]) % device_total]
    placed = (owner_slot * REQ_DEV + local_index).astype(jnp.int32)
    holders = jnp.zeros((REQUESTS,), jnp.int32).at[placed].set(request_ids)
    return (placed, holders)


def draw_prompt_place(key, part):
    return placement(key)[0]


def draw_owned_request(key, part):
    return placement(key)[1]


def plant(values, rng, low, top_value):
    dims = values.shape
    index_at = [jax.random.randint(jax.random.fold_in(rng, axis), (), 0, dims[axis]) for axis in range(len(dims))]
    values = values.at[tuple(index_at)].set(low)
    longest = dims.index(max(dims))
    index_at[longest] = (index_at[longest] + 1) % dims[longest]
    return values.at[tuple(index_at)].set(top_value)


def levels(own_key, extent, pieces, smallest, largest):
    def one(position, parts):
        draws = jax.random.uniform(jax.random.fold_in(jax.random.fold_in(own_key, 6), position), (parts,), jnp.float32, smallest / len(pieces), largest / len(pieces))
        return jnp.repeat(jnp.exp(draws), extent[position] // parts).reshape((-1,) + (1,) * (len(extent) - position - 1))

    factor_of = one(*pieces[0])
    for cut in pieces[1:]:
        factor_of = factor_of * one(*cut)
    return factor_of


def scatter_about(rng, shape, width, most, pieces=(), held_as=jnp.bfloat16):
    values = width * jax.random.normal(rng, shape, jnp.float32)
    if pieces:
        values = values * levels(rng, shape, pieces, -0.22, 0.18)
    return jnp.clip(values, -most, most).astype(held_as)


def setup_inputs(seed: int = 0) -> dict:
    splits = jax.random.split(jax.random.key(seed), 15)
    return {
        "queries": draw_queries(jax.random.fold_in(splits[14], 71), 0),
        "new_kv": scatter_about(splits[1], (STEPS, ROWS, 2, HEADS * HEAD_DIM), 1.0, 4.0, ((1, 64), (3, 8))),
        "residual": scatter_about(splits[2], (STEPS, ROWS, D), 0.3, 1.1953125, ((1, 64),)),
        "home_cache": draw_home_cache(jax.random.fold_in(splits[14], 71), 0),
        "prompt_cache": draw_prompt_cache(jax.random.fold_in(splits[14], 71), 0),
        "home_table": plant(jax.random.randint(splits[5], (ROWS, HOME_BLOCKS), 0, POOL_DEV), jax.random.fold_in(splits[5], 1), 0, POOL_DEV - 1).astype(jnp.int32),
        "home_len": draw_home_len(jax.random.fold_in(splits[14], 71), 0),
        "parents": plant(jax.random.randint(splits[7], (STEPS, ROWS), 0, BEAMS), jax.random.fold_in(splits[7], 1), 0, BEAMS - 1).astype(jnp.int32),
        "prompt_place": draw_prompt_place(jax.random.fold_in(splits[14], 71), 0),
        "owned_request": draw_owned_request(jax.random.fold_in(splits[14], 71), 0),
        "prompt_len": draw_prompt_len(jax.random.fold_in(splits[14], 71), 0),
        "out_weight": scatter_about(splits[11], (HEADS * HEAD_DIM, D), (HEADS * HEAD_DIM) ** -0.5, 0.1875, ((0, 8),)),
        "norm_gain": jnp.clip(1.0 + 0.18 * jax.random.normal(splits[12], (D,), jnp.float32), 0.099609375, 1.8984375).astype(jnp.bfloat16),
        "qkv_weight": scatter_about(splits[13], (D, 3, HEADS * HEAD_DIM), (16 * D) ** -0.5, 0.03125, ((2, 8),)),
    }


NEG_FILL = -1e+30
NORM_EPS = 1e-05

def reference(queries, new_kv, residual, home_cache, prompt_cache, home_table, home_len, parents, prompt_place, owned_request, prompt_len, out_weight, norm_gain, qkv_weight):
    lane_width = HEADS * HEAD_DIM
    row_count = queries.shape[1]
    request_count = row_count // BEAMS
    score_scale = 1.0 / math.sqrt(HEAD_DIM)
    row_index = jnp.arange(row_count, dtype=jnp.int32)
    request_base = row_index // BEAMS * BEAMS
    device_of_row = row_index // BEAMS_DEV
    tables = home_table + (device_of_row * POOL_DEV)[:, None]
    first_parent = request_base + parents[0]
    tables = tables[first_parent]
    lengths = home_len[first_parent]
    window = jnp.zeros((row_count, STEPS, 2, lane_width), jnp.bfloat16)
    prompt_tokens = PROMPT_BLOCKS * BLOCK
    home_tokens = HOME_BLOCKS * BLOCK
    prompts = prompt_cache.reshape(REQUESTS, prompt_tokens, 2, lane_width)
    live_prompt = prompt_len[prompt_place]
    prompt_asker = owned_request[prompt_place]
    prompt_pos = jnp.arange(prompt_tokens, dtype=jnp.int32)
    home_pos = jnp.arange(home_tokens, dtype=jnp.int32)
    window_pos = jnp.arange(STEPS, dtype=jnp.int32)
    gain_row = norm_gain.astype(jnp.float32)
    weight_flat = qkv_weight.reshape(D, 3 * lane_width)
    qkv_list = []
    residual_list = []
    for step_index in range(STEPS):
        if step_index > 0:
            window = window.at[:, step_index - 1].set(new_kv[step_index - 1])
            chosen = request_base + parents[step_index]
            window = window[chosen]
            tables = tables[chosen]
            lengths = lengths[chosen]
        step_queries = queries[step_index].reshape(request_count, BEAMS, lane_width)

        def attend(item_parts):
            query_rows, asker_rows, table_rows, length_rows, window_rows, own_rows, prompt_slot, prompt_live = item_parts
            query_heads = query_rows.reshape(BEAMS, HEADS, HEAD_DIM).astype(jnp.float32)
            asker_heads = asker_rows.reshape(BEAMS, HEADS, HEAD_DIM).astype(jnp.float32)
            prompt_rows = lax.dynamic_index_in_dim(prompts, prompt_slot, 0, keepdims=False)
            prompt_rows = prompt_rows.reshape(prompt_tokens, 2, HEADS, HEAD_DIM).astype(jnp.float32)
            home_rows = home_cache[table_rows].reshape(BEAMS, home_tokens, 2, HEADS, HEAD_DIM).astype(jnp.float32)
            window_heads = window_rows.reshape(BEAMS, STEPS, 2, HEADS, HEAD_DIM).astype(jnp.float32)
            own_heads = own_rows.reshape(BEAMS, 2, HEADS, HEAD_DIM).astype(jnp.float32)
            prompt_scores = jnp.einsum('bhd,thd->bht', asker_heads, prompt_rows[:, 0]) * score_scale
            prompt_scores = jnp.where(prompt_pos < prompt_live, prompt_scores, NEG_FILL)
            home_scores = jnp.einsum('bhd,bthd->bht', query_heads, home_rows[:, :, 0]) * score_scale
            home_scores = jnp.where(home_pos[None, None, :] < length_rows[:, None, None], home_scores, NEG_FILL)
            window_scores = jnp.einsum('bhd,bthd->bht', query_heads, window_heads[:, :, 0]) * score_scale
            window_scores = jnp.where(window_pos < step_index, window_scores, NEG_FILL)
            own_scores = jnp.einsum('bhd,bhd->bh', query_heads, own_heads[:, 0])[:, :, None] * score_scale
            scores = jnp.concatenate([prompt_scores, home_scores, window_scores, own_scores], axis=-1)
            row_top = lax.optimization_barrier(jnp.max(scores, axis=-1, keepdims=True))
            weights = jnp.exp(scores - row_top).astype(jnp.bfloat16)
            weights = lax.optimization_barrier(weights).astype(jnp.float32)
            weight_sum = lax.optimization_barrier(jnp.sum(weights, axis=-1))
            split_one = prompt_tokens
            split_two = prompt_tokens + home_tokens
            numerator = jnp.einsum('bht,thd->bhd', weights[:, :, :split_one], prompt_rows[:, 1])
            numerator = numerator + jnp.einsum('bht,bthd->bhd', weights[:, :, split_one:split_two], home_rows[:, :, 1])
            numerator = numerator + jnp.einsum('bht,bthd->bhd', weights[:, :, split_two:split_two + STEPS], window_heads[:, :, 1])
            numerator = numerator + weights[:, :, -1:] * own_heads[:, 1]
            return (numerator / weight_sum[:, :, None]).astype(jnp.bfloat16).reshape(BEAMS, lane_width)
        attended = lax.map(attend, (step_queries, step_queries[prompt_asker], tables.reshape(request_count, BEAMS, HOME_BLOCKS), lengths.reshape(request_count, BEAMS), window.reshape(request_count, BEAMS, STEPS, 2, lane_width), new_kv[step_index].reshape(request_count, BEAMS, 2, lane_width), prompt_place, live_prompt)).reshape(row_count, lane_width)
        mixed_rows = residual[step_index].astype(jnp.float32) + jnp.dot(attended, out_weight, preferred_element_type=jnp.float32)
        residual_list.append(mixed_rows.astype(jnp.bfloat16))
        mean_square = lax.optimization_barrier(jnp.mean(mixed_rows * mixed_rows, axis=-1, keepdims=True))
        normed = (mixed_rows * lax.rsqrt(mean_square + NORM_EPS) * gain_row).astype(jnp.bfloat16)
        projected = jnp.dot(normed, weight_flat, preferred_element_type=jnp.float32).astype(jnp.bfloat16)
        qkv_list.append(projected.reshape(row_count, 3, lane_width))
    return (jnp.stack(qkv_list), jnp.stack(residual_list))
```

```python
import math

import jax
import jax.numpy as jnp
from jax import lax
from jax.experimental import pallas as pl
from jax.experimental.pallas import tpu as pltpu
from jax.sharding import PartitionSpec as P

HEAD_DIM = 64
BEAMS = 8

NEG_FILL = -1e30
NORM_EPS = 1e-05
SCORE_SCALE = 1.0 / math.sqrt(HEAD_DIM)
LANES = 2 * HEAD_DIM
STAT_ROWS = 8


def split_heads(rows):
    lane = lax.broadcasted_iota(jnp.int32, rows.shape, 1)
    zero = jnp.zeros_like(rows)
    return jnp.concatenate(
        [jnp.where(lane < HEAD_DIM, rows, zero), jnp.where(lane >= HEAD_DIM, rows, zero)], axis=0
    )


def join_heads(rows):
    half = rows.shape[0] // 2
    lane = lax.broadcasted_iota(jnp.int32, (half, rows.shape[1]), 1)
    return jnp.where(lane < HEAD_DIM, rows[:half], rows[half:])


def dot_rows(left, right):
    return lax.dot_general(
        left, right, (((1,), (1,)), ((), ())), preferred_element_type=jnp.float32
    )


def to_value_rows(weights):
    return pltpu.roll(weights, 1, axis=1).astype(jnp.bfloat16)


def prompt_kernel(owned_ref, live_ref, held_ref, cache_ref, out_ref, query_ref, sem):
    owner = owned_ref[0]
    chips = held_ref.shape[0] // 2
    slot = (owner % 2) * chips + owner // 2
    copy = pltpu.make_async_copy(held_ref.at[slot], query_ref, sem)
    copy.start()
    copy.wait()
    rows = query_ref.shape[0]
    queries = split_heads(query_ref[...])
    cache = cache_ref[...]
    scores = dot_rows(queries, cache) * SCORE_SCALE
    column = lax.broadcasted_iota(jnp.int32, scores.shape, 1)
    valid = jnp.logical_and(column % 2 == 0, column < 2 * live_ref[0])
    scores = jnp.where(valid, scores, NEG_FILL)
    top = jnp.max(scores, axis=1, keepdims=True)
    weights = jnp.exp(scores - top).astype(jnp.bfloat16).astype(jnp.float32)
    total = jnp.sum(weights, axis=1, keepdims=True)
    numer = jnp.dot(to_value_rows(weights), cache, preferred_element_type=jnp.float32)
    mean = join_heads(numer / total).astype(jnp.bfloat16)
    level = top + jnp.log(total)
    high = level.astype(jnp.bfloat16).astype(jnp.float32)
    rest = level - high
    middle = rest.astype(jnp.bfloat16).astype(jnp.float32)
    low = rest - middle
    wide = (2 * rows, LANES)
    lane = lax.broadcasted_iota(jnp.int32, wide, 1)
    row = lax.broadcasted_iota(jnp.int32, wide, 0)
    on_row = lane % HEAD_DIM == row
    first = jnp.sum(
        jnp.where(on_row, jnp.where(lane < HEAD_DIM, high, middle), 0.0), axis=0, keepdims=True
    )
    second = jnp.sum(jnp.where(on_row, low, 0.0), axis=0, keepdims=True)
    stat_row = lax.broadcasted_iota(jnp.int32, (STAT_ROWS, LANES), 0)
    stats = jnp.where(stat_row == 0, first, jnp.where(stat_row == 1, second, 0.0))
    packet = jnp.concatenate([mean.astype(jnp.float32), stats], axis=0).astype(jnp.bfloat16)
    for index in range(out_ref.shape[0]):
        out_ref[index] = packet


def home_kernel(
    place_ref,
    table_ref,
    length_ref,
    parent_ref,
    query_ref,
    home_ref,
    fresh_ref,
    result_ref,
    out_ref,
    root_ref,
    line_ref,
    packet_ref,
    sem,
):
    place = place_ref[0]
    chips = result_ref.shape[0] // 2
    slot = (place % 2) * chips + place // 2
    copy = pltpu.make_async_copy(result_ref.at[slot], packet_ref, sem)
    copy.start()
    step_count = parent_ref.shape[0]
    block_count = table_ref.shape[0]
    rows = query_ref.shape[0]
    block_tokens = home_ref.shape[0] // (2 * block_count)
    unit = (BEAMS, LANES)
    beam_row = lax.broadcasted_iota(jnp.int32, unit, 0)
    lane = lax.broadcasted_iota(jnp.int32, unit, 1)
    is_key = lane % 2 == 0
    half_lane = lane // 2

    def column_of(values):
        built = jnp.full(unit, values[0], jnp.int32)
        for beam in range(1, BEAMS):
            built = jnp.where(beam_row == beam, values[beam], built)
        return built

    counts = []
    fresh_masks = []
    for step in range(step_count):
        roots = []
        for beam in range(BEAMS):
            parent = parent_ref[step, beam]
            root = parent if step == 0 else root_ref[step - 1, parent]
            root_ref[step, beam] = root
            roots.append(root)
            line_ref[step * step_count + step, beam] = beam
            for source in range(step):
                line_ref[step * step_count + source, beam] = line_ref[
                    (step - 1) * step_count + source, parent
                ]
        length = column_of([length_ref[root] for root in roots])
        entries = [
            column_of([table_ref[entry, root] for root in roots]) for entry in range(block_count)
        ]
        pieces = []
        for block in range(block_count):
            limits = [
                jnp.where(entries[entry] == block, length - entry * block_tokens, 0)
                for entry in range(block_count)
            ]
            for part in range(2 * block_tokens // LANES):
                offset = half_lane + part * (LANES // 2)
                count = jnp.zeros(unit, jnp.float32)
                for limit in limits:
                    count = count + jnp.where(offset < limit, 1.0, 0.0)
                pieces.append(jnp.where(is_key, count, 0.0))
        counts.append(jnp.concatenate(pieces, axis=1))
        seen = jnp.zeros(unit, jnp.float32)
        for source in range(step + 1):
            if source == step:
                target = beam_row + source * BEAMS
            else:
                target = (
                    column_of([line_ref[step * step_count + source, beam] for beam in range(BEAMS)])
                    + source * BEAMS
                )
            seen = jnp.where(half_lane == target, 1.0, seen)
        fresh_masks.append(jnp.where(is_key, seen, 0.0))
    count = jnp.concatenate(counts * 2, axis=0)
    fresh_mask = jnp.concatenate(fresh_masks * 2, axis=0)

    queries = split_heads(query_ref[...])
    home = home_ref[...]
    fresh = fresh_ref[...]
    fresh = jnp.concatenate(
        [fresh, jnp.zeros((LANES - fresh.shape[0], LANES), fresh.dtype)], axis=0
    )
    scores = jnp.where(count > 0.0, dot_rows(queries, home) * SCORE_SCALE, NEG_FILL)
    fresh_scores = jnp.where(fresh_mask > 0.0, dot_rows(queries, fresh) * SCORE_SCALE, NEG_FILL)
    top = jnp.maximum(
        jnp.max(scores, axis=1, keepdims=True), jnp.max(fresh_scores, axis=1, keepdims=True)
    )
    weights = jnp.exp(scores - top).astype(jnp.bfloat16).astype(jnp.float32) * count
    weights = weights.astype(jnp.bfloat16).astype(jnp.float32)
    fresh_weights = jnp.exp(fresh_scores - top).astype(jnp.bfloat16).astype(jnp.float32)
    total = jnp.sum(weights, axis=1, keepdims=True) + jnp.sum(fresh_weights, axis=1, keepdims=True)
    numer = jnp.dot(to_value_rows(weights), home, preferred_element_type=jnp.float32)
    numer = numer + jnp.dot(
        to_value_rows(fresh_weights), fresh, preferred_element_type=jnp.float32
    )

    copy.wait()
    packet = packet_ref[...].astype(jnp.float32)
    mean = packet[:rows]
    wide = (2 * rows, LANES)
    wide_lane = lax.broadcasted_iota(jnp.int32, wide, 1)
    wide_row = lax.broadcasted_iota(jnp.int32, wide, 0)
    on_row = wide_lane % HEAD_DIM == wide_row
    low_half = wide_lane < HEAD_DIM
    level = jnp.sum(
        jnp.where(on_row, jnp.broadcast_to(packet[rows : rows + 1], wide), 0.0),
        axis=1,
        keepdims=True,
    ) + jnp.sum(
        jnp.where(
            jnp.logical_and(on_row, low_half),
            jnp.broadcast_to(packet[rows + 1 : rows + 2], wide),
            0.0,
        ),
        axis=1,
        keepdims=True,
    )
    joint_top = jnp.maximum(top, level)
    home_factor = jnp.exp(top - joint_top)
    prompt_factor = jnp.exp(level - joint_top)
    both = jnp.concatenate([mean, mean], axis=0)
    attended = (numer * home_factor + both * prompt_factor) / (
        total * home_factor + prompt_factor
    )
    attended = join_heads(attended).astype(jnp.bfloat16)
    for index in range(out_ref.shape[0]):
        out_ref[index] = attended


def mix_kernel(
    attended_ref, weight_ref, residual_ref, gain_ref, qkv_weight_ref, qkv_ref, residual_out_ref
):
    shard_count = attended_ref.shape[0]
    attended = jnp.concatenate([attended_ref[index] for index in range(shard_count)], axis=1)
    mixed = residual_ref[...].astype(jnp.float32) + jnp.dot(
        attended, weight_ref[...], preferred_element_type=jnp.float32
    )
    residual_out_ref[...] = mixed.astype(jnp.bfloat16)
    mean_square = jnp.mean(mixed * mixed, axis=1, keepdims=True)
    gain = gain_ref[...].astype(jnp.float32)
    normed = (mixed * lax.rsqrt(mean_square + NORM_EPS) * gain).astype(jnp.bfloat16)
    for kind in range(qkv_weight_ref.shape[0]):
        projected = jnp.dot(
            normed, qkv_weight_ref[kind], preferred_element_type=jnp.float32
        ).astype(jnp.bfloat16)
        for step in range(qkv_ref.shape[0]):
            qkv_ref[step, kind] = projected[step * BEAMS : (step + 1) * BEAMS]


VMEM_SPEC = pl.BlockSpec(memory_space=pltpu.VMEM)
SMEM_SPEC = pl.BlockSpec(memory_space=pltpu.SMEM)
ANY_SPEC = pl.BlockSpec(memory_space=pl.ANY)


def shards(
    queries,
    new_kv,
    residual,
    home_cache,
    prompt_cache,
    home_table,
    home_len,
    parents,
    prompt_place,
    owned_request,
    prompt_len,
    out_weight,
    norm_gain,
    qkv_weight,
):
    step_count, row_count, lane_count = queries.shape
    model_width = residual.shape[-1]
    rows = step_count * row_count
    req_size = lax.axis_size("req")
    tp_size = lax.axis_size("tp")
    chips = req_size // 2
    same_core = [[2 * chip + core for chip in range(chips)] for core in range(2)]
    same_chip = [[2 * chip, 2 * chip + 1] for chip in range(chips)]

    def route(slots):
        arrived = lax.all_to_all(slots, "req", 0, 0, axis_index_groups=same_core)
        return lax.all_gather(arrived, "req", axis_index_groups=same_chip, tiled=True)

    whole_weight = lax.all_gather(out_weight, "tp", axis=0, tiled=True)

    query_rows = queries.reshape(rows, lane_count)
    held = route(jnp.broadcast_to(query_rows[None], (chips, rows, lane_count)))
    prompt_rows = prompt_cache.reshape(-1, lane_count)
    packet_rows = rows + STAT_ROWS
    results = pl.pallas_call(
        prompt_kernel,
        out_shape=jax.ShapeDtypeStruct((chips, packet_rows, lane_count), jnp.bfloat16),
        in_specs=[SMEM_SPEC, SMEM_SPEC, ANY_SPEC, VMEM_SPEC],
        out_specs=VMEM_SPEC,
        scratch_shapes=[pltpu.VMEM((rows, lane_count), jnp.bfloat16), pltpu.SemaphoreType.DMA],
        name="prompt_attention",
    )(owned_request, prompt_len, held, prompt_rows)
    returned = route(results)

    home_rows = home_cache.reshape(-1, lane_count)
    fresh_rows = new_kv.reshape(-1, lane_count)
    attended = pl.pallas_call(
        home_kernel,
        out_shape=jax.ShapeDtypeStruct((tp_size, rows, lane_count), jnp.bfloat16),
        in_specs=[SMEM_SPEC] * 4 + [VMEM_SPEC] * 3 + [ANY_SPEC],
        out_specs=VMEM_SPEC,
        scratch_shapes=[
            pltpu.SMEM((step_count, BEAMS), jnp.int32),
            pltpu.SMEM((step_count * step_count, BEAMS), jnp.int32),
            pltpu.VMEM((packet_rows, lane_count), jnp.bfloat16),
            pltpu.SemaphoreType.DMA,
        ],
        name="home_attention",
    )(
        prompt_place,
        home_table.T,
        home_len,
        parents,
        query_rows,
        home_rows,
        fresh_rows,
        returned,
    )
    all_heads = lax.all_to_all(attended, "tp", 0, 0)
    next_qkv, new_residual = pl.pallas_call(
        mix_kernel,
        out_shape=(
            jax.ShapeDtypeStruct((step_count, 3, row_count, lane_count), jnp.bfloat16),
            jax.ShapeDtypeStruct((rows, model_width), jnp.bfloat16),
        ),
        in_specs=[VMEM_SPEC] * 5,
        out_specs=(VMEM_SPEC, VMEM_SPEC),
        compiler_params=pltpu.CompilerParams(vmem_limit_bytes=40 * 1024 * 1024),
        name="mix",
    )(
        all_heads,
        whole_weight,
        residual.reshape(rows, model_width),
        norm_gain.reshape(1, model_width),
        qkv_weight.transpose(1, 0, 2),
    )
    return (
        next_qkv.transpose(0, 2, 1, 3),
        new_residual.reshape(step_count, row_count, model_width),
    )


def solution(mesh):
    placed = (
        P(None, "req", "tp"),
        P(None, "req", None, "tp"),
        P(None, "req", None),
        P("req", None, None, "tp"),
        P("req", None, None, "tp"),
        P("req", None),
        P("req"),
        P(None, "req"),
        P("req"),
        P("req"),
        P("req"),
        P("tp", None),
        P(),
        P(None, None, "tp"),
    )
    return jax.shard_map(
        shards,
        mesh=mesh,
        in_specs=placed,
        out_specs=(P(None, "req", None, "tp"), P(None, "req", None)),
        check_vma=False,
    )
```

```python
import math

import jax
import jax.numpy as jnp
from jax import lax
from jax.experimental import pallas as pl
from jax.experimental.pallas import tpu as pltpu
from jax.sharding import PartitionSpec as P

HEAD_DIM = 64
BEAMS = 8

NEG_FILL = -1e30
NORM_EPS = 1e-05
SCORE_SCALE = 1.0 / math.sqrt(HEAD_DIM)
LANES = 2 * HEAD_DIM
STAT_ROWS = 8
NOTE_ROWS = 16


def split_heads(rows):
    lane = lax.broadcasted_iota(jnp.int32, rows.shape, 1)
    zero = jnp.zeros_like(rows)
    return jnp.concatenate(
        [jnp.where(lane < HEAD_DIM, rows, zero), jnp.where(lane >= HEAD_DIM, rows, zero)], axis=0
    )


def join_heads(rows):
    half = rows.shape[0] // 2
    lane = lax.broadcasted_iota(jnp.int32, (half, rows.shape[1]), 1)
    return jnp.where(lane < HEAD_DIM, rows[:half], rows[half:])


def dot_rows(left, right):
    return lax.dot_general(
        left, right, (((1,), (1,)), ((), ())), preferred_element_type=jnp.float32
    )


def to_value_rows(weights):
    return pltpu.roll(weights, 1, axis=1).astype(jnp.bfloat16)


def prompt_kernel(asked_ref, slots_ref, out_ref):
    core = lax.axis_index("req") % 2
    rows = asked_ref.shape[1]
    tokens = slots_ref.shape[1] - NOTE_ROWS
    lane = lax.broadcasted_iota(jnp.int32, (NOTE_ROWS, LANES), 1)
    row = lax.broadcasted_iota(jnp.int32, (NOTE_ROWS, LANES), 0)
    for slot in range(2):
        note = slots_ref[slot, tokens:].astype(jnp.float32)

        def number(index):
            here = jnp.logical_and(row == 0, lane == index)
            return jnp.sum(jnp.where(here, note, 0.0)).astype(jnp.int32)

        owner = number(0)
        live = number(1) * 16 + number(2)

        @pl.when(owner % 2 == core)
        def _():
            chip = owner // 2
            out_ref[chip] = prompt_packet(asked_ref[chip], slots_ref[slot, :tokens], live, rows)


def prompt_packet(query_rows, cache, live, rows):
    queries = split_heads(query_rows)
    scores = dot_rows(queries, cache) * SCORE_SCALE
    column = lax.broadcasted_iota(jnp.int32, scores.shape, 1)
    valid = jnp.logical_and(column % 2 == 0, column < 2 * live)
    scores = jnp.where(valid, scores, NEG_FILL)
    top = jnp.max(scores, axis=1, keepdims=True)
    weights = jnp.exp(scores - top).astype(jnp.bfloat16).astype(jnp.float32)
    total = jnp.sum(weights, axis=1, keepdims=True)
    numer = jnp.dot(to_value_rows(weights), cache, preferred_element_type=jnp.float32)
    mean = join_heads(numer / total).astype(jnp.bfloat16)
    level = top + jnp.log(total)
    high = level.astype(jnp.bfloat16).astype(jnp.float32)
    rest = level - high
    middle = rest.astype(jnp.bfloat16).astype(jnp.float32)
    low = rest - middle
    wide = (2 * rows, LANES)
    lane = lax.broadcasted_iota(jnp.int32, wide, 1)
    row = lax.broadcasted_iota(jnp.int32, wide, 0)
    on_row = lane % HEAD_DIM == row
    first = jnp.sum(
        jnp.where(on_row, jnp.where(lane < HEAD_DIM, high, middle), 0.0), axis=0, keepdims=True
    )
    second = jnp.sum(jnp.where(on_row, low, 0.0), axis=0, keepdims=True)
    stat_row = lax.broadcasted_iota(jnp.int32, (STAT_ROWS, LANES), 0)
    stats = jnp.where(stat_row == 0, first, jnp.where(stat_row == 1, second, 0.0))
    return jnp.concatenate([mean.astype(jnp.float32), stats], axis=0).astype(jnp.bfloat16)


def home_kernel(
    owned_ref,
    live_ref,
    table_ref,
    length_ref,
    parent_ref,
    query_ref,
    home_ref,
    fresh_ref,
    prompt_ref,
    mean_ref,
    level_ref,
    slot_ref,
    root_ref,
    line_ref,
    note_ref,
    sems,
):
    tokens = prompt_ref.shape[0]
    note_lane = lax.broadcasted_iota(jnp.int32, (NOTE_ROWS, LANES), 1)
    live = live_ref[0]
    note = jnp.where(
        note_lane == 0, owned_ref[0], jnp.where(note_lane == 1, live // 16, live % 16)
    )
    note_ref[...] = note.astype(jnp.float32).astype(jnp.bfloat16)
    copies = [
        pltpu.make_async_copy(prompt_ref, slot_ref.at[pl.ds(0, tokens)], sems.at[0]),
        pltpu.make_async_copy(note_ref, slot_ref.at[pl.ds(tokens, NOTE_ROWS)], sems.at[1]),
    ]
    for copy in copies:
        copy.start()
    step_count = parent_ref.shape[0]
    block_count = table_ref.shape[0]
    rows = query_ref.shape[0]
    block_tokens = home_ref.shape[0] // (2 * block_count)
    unit = (BEAMS, LANES)
    beam_row = lax.broadcasted_iota(jnp.int32, unit, 0)
    lane = lax.broadcasted_iota(jnp.int32, unit, 1)
    is_key = lane % 2 == 0
    half_lane = lane // 2

    def column_of(values):
        built = jnp.full(unit, values[0], jnp.int32)
        for beam in range(1, BEAMS):
            built = jnp.where(beam_row == beam, values[beam], built)
        return built

    counts = []
    fresh_masks = []
    for step in range(step_count):
        roots = []
        for beam in range(BEAMS):
            parent = parent_ref[step, beam]
            root = parent if step == 0 else root_ref[step - 1, parent]
            root_ref[step, beam] = root
            roots.append(root)
            line_ref[step * step_count + step, beam] = beam
            for source in range(step):
                line_ref[step * step_count + source, beam] = line_ref[
                    (step - 1) * step_count + source, parent
                ]
        length = column_of([length_ref[root] for root in roots])
        entries = [
            column_of([table_ref[entry, root] for root in roots]) for entry in range(block_count)
        ]
        pieces = []
        for block in range(block_count):
            limits = [
                jnp.where(entries[entry] == block, length - entry * block_tokens, 0)
                for entry in range(block_count)
            ]
            for part in range(2 * block_tokens // LANES):
                offset = half_lane + part * (LANES // 2)
                count = jnp.zeros(unit, jnp.float32)
                for limit in limits:
                    count = count + jnp.where(offset < limit, 1.0, 0.0)
                pieces.append(jnp.where(is_key, count, 0.0))
        counts.append(jnp.concatenate(pieces, axis=1))
        seen = jnp.zeros(unit, jnp.float32)
        for source in range(step + 1):
            if source == step:
                target = beam_row + source * BEAMS
            else:
                target = (
                    column_of([line_ref[step * step_count + source, beam] for beam in range(BEAMS)])
                    + source * BEAMS
                )
            seen = jnp.where(half_lane == target, 1.0, seen)
        fresh_masks.append(jnp.where(is_key, seen, 0.0))
    count = jnp.concatenate(counts * 2, axis=0)
    fresh_mask = jnp.concatenate(fresh_masks * 2, axis=0)

    queries = split_heads(query_ref[...])
    home = home_ref[...]
    fresh = fresh_ref[...]
    fresh = jnp.concatenate(
        [fresh, jnp.zeros((LANES - fresh.shape[0], LANES), fresh.dtype)], axis=0
    )
    scores = jnp.where(count > 0.0, dot_rows(queries, home) * SCORE_SCALE, NEG_FILL)
    fresh_scores = jnp.where(fresh_mask > 0.0, dot_rows(queries, fresh) * SCORE_SCALE, NEG_FILL)
    top = jnp.maximum(
        jnp.max(scores, axis=1, keepdims=True), jnp.max(fresh_scores, axis=1, keepdims=True)
    )
    weights = jnp.exp(scores - top).astype(jnp.bfloat16).astype(jnp.float32) * count
    weights = weights.astype(jnp.bfloat16).astype(jnp.float32)
    fresh_weights = jnp.exp(fresh_scores - top).astype(jnp.bfloat16).astype(jnp.float32)
    total = jnp.sum(weights, axis=1, keepdims=True) + jnp.sum(fresh_weights, axis=1, keepdims=True)
    numer = jnp.dot(to_value_rows(weights), home, preferred_element_type=jnp.float32)
    numer = numer + jnp.dot(
        to_value_rows(fresh_weights), fresh, preferred_element_type=jnp.float32
    )

    mean_ref[...] = join_heads(numer / total)
    level = jnp.broadcast_to(top + jnp.log(total), numer.shape)
    level_ref[...] = join_heads(level)
    for copy in copies:
        copy.wait()


def combine_kernel(place_ref, mean_ref, level_ref, result_ref, weight_ref, out_ref):
    rows = mean_ref.shape[0]
    packet = result_ref[place_ref[0] // 2].astype(jnp.float32)
    wide = (2 * rows, LANES)
    lane = lax.broadcasted_iota(jnp.int32, wide, 1)
    row = lax.broadcasted_iota(jnp.int32, wide, 0)
    on_row = lane % HEAD_DIM == row
    terms = jnp.broadcast_to(packet[rows : rows + 1], wide) + jnp.where(
        lane < HEAD_DIM, jnp.broadcast_to(packet[rows + 1 : rows + 2], wide), 0.0
    )
    prompt_level = jnp.sum(jnp.where(on_row, terms, 0.0), axis=1, keepdims=True)
    prompt_level = join_heads(jnp.broadcast_to(prompt_level, wide))
    level = level_ref[...]
    joint_top = jnp.maximum(level, prompt_level)
    home_factor = jnp.exp(level - joint_top)
    prompt_factor = jnp.exp(prompt_level - joint_top)
    attended = (mean_ref[...] * home_factor + packet[:rows] * prompt_factor) / (
        home_factor + prompt_factor
    )
    partial = jnp.dot(
        attended.astype(jnp.bfloat16), weight_ref[...], preferred_element_type=jnp.float32
    )
    width = out_ref.shape[2]
    for index in range(out_ref.shape[0]):
        out_ref[index] = partial[:, index * width : (index + 1) * width].astype(out_ref.dtype)


def sum_kernel(partial_ref, residual_ref, out_ref):
    width = partial_ref.shape[2]
    first = pl.multiple_of(lax.axis_index("tp") * width, width)
    mixed = residual_ref[:, pl.ds(first, width)].astype(jnp.float32)
    for index in range(partial_ref.shape[0]):
        mixed = mixed + partial_ref[index].astype(jnp.float32)
    mixed = mixed.astype(jnp.bfloat16)
    for index in range(out_ref.shape[0]):
        out_ref[index] = mixed


def project_kernel(mixed_ref, gain_ref, qkv_weight_ref, qkv_ref, residual_out_ref):
    shard_count = mixed_ref.shape[0]
    rounded = jnp.concatenate([mixed_ref[index] for index in range(shard_count)], axis=1)
    residual_out_ref[...] = rounded
    mixed = rounded.astype(jnp.float32)
    mean_square = jnp.mean(mixed * mixed, axis=1, keepdims=True)
    gain = gain_ref[...].astype(jnp.float32)
    normed = (mixed * lax.rsqrt(mean_square + NORM_EPS) * gain).astype(jnp.bfloat16)
    for kind in range(qkv_weight_ref.shape[0]):
        projected = jnp.dot(
            normed, qkv_weight_ref[kind], preferred_element_type=jnp.float32
        ).astype(jnp.bfloat16)
        for step in range(qkv_ref.shape[0]):
            qkv_ref[step, kind] = projected[step * BEAMS : (step + 1) * BEAMS]


VMEM_SPEC = pl.BlockSpec(memory_space=pltpu.VMEM)
SMEM_SPEC = pl.BlockSpec(memory_space=pltpu.SMEM)
KERNEL_PARAMS = pltpu.CompilerParams(vmem_limit_bytes=20 * 1024 * 1024)
ANY_SPEC = pl.BlockSpec(memory_space=pl.ANY)


def shards(
    queries,
    new_kv,
    residual,
    home_cache,
    prompt_cache,
    home_table,
    home_len,
    parents,
    prompt_place,
    owned_request,
    prompt_len,
    out_weight,
    norm_gain,
    qkv_weight,
):
    step_count, row_count, lane_count = queries.shape
    model_width = residual.shape[-1]
    rows = step_count * row_count
    req_size = lax.axis_size("req")
    tp_size = lax.axis_size("tp")
    chips = req_size // 2
    same_core = [[2 * chip + core for chip in range(chips)] for core in range(2)]
    same_chip = [[2 * chip, 2 * chip + 1] for chip in range(chips)]

    def route(slots):
        return lax.all_to_all(slots, "req", 0, 0, axis_index_groups=same_core)

    query_rows = queries.reshape(rows, lane_count)
    asked = route(jnp.broadcast_to(query_rows[None], (chips, rows, lane_count)))

    home_rows = home_cache.reshape(-1, lane_count)
    fresh_rows = new_kv.reshape(-1, lane_count)
    prompt_rows = prompt_cache.reshape(-1, lane_count)
    slot_rows = prompt_rows.shape[0] + NOTE_ROWS
    home_mean, home_level, own_slot = pl.pallas_call(
        home_kernel,
        out_shape=(
            jax.ShapeDtypeStruct((rows, lane_count), jnp.float32),
            jax.ShapeDtypeStruct((rows, lane_count), jnp.float32),
            jax.ShapeDtypeStruct((slot_rows, lane_count), jnp.bfloat16),
        ),
        in_specs=[SMEM_SPEC] * 5 + [VMEM_SPEC] * 3 + [ANY_SPEC],
        out_specs=(VMEM_SPEC, VMEM_SPEC, ANY_SPEC),
        scratch_shapes=[
            pltpu.SMEM((step_count, BEAMS), jnp.int32),
            pltpu.SMEM((step_count * step_count, BEAMS), jnp.int32),
            pltpu.VMEM((NOTE_ROWS, lane_count), jnp.bfloat16),
            pltpu.SemaphoreType.DMA((2,)),
        ],
        compiler_params=KERNEL_PARAMS,
        name="home_attention",
    )(
        owned_request,
        prompt_len,
        home_table.T,
        home_len,
        parents,
        query_rows,
        home_rows,
        fresh_rows,
        prompt_rows,
    )
    both_slots = lax.all_gather(own_slot, "req", axis_index_groups=same_chip)

    packet_rows = rows + STAT_ROWS
    results = pl.pallas_call(
        prompt_kernel,
        out_shape=jax.ShapeDtypeStruct((chips, packet_rows, lane_count), jnp.bfloat16),
        in_specs=[VMEM_SPEC] * 2,
        out_specs=VMEM_SPEC,
        compiler_params=KERNEL_PARAMS,
        name="prompt_attention",
    )(asked, both_slots)
    returned = route(results)

    width = model_width // tp_size
    partial = pl.pallas_call(
        combine_kernel,
        out_shape=jax.ShapeDtypeStruct((tp_size, rows, width), jnp.float32),
        in_specs=[SMEM_SPEC] + [VMEM_SPEC] * 4,
        out_specs=VMEM_SPEC,
        compiler_params=KERNEL_PARAMS,
        name="combine",
    )(prompt_place, home_mean, home_level, returned, out_weight)
    partials = lax.all_to_all(partial, "tp", 0, 0)
    mixed = pl.pallas_call(
        sum_kernel,
        out_shape=jax.ShapeDtypeStruct((tp_size, rows, width), jnp.bfloat16),
        in_specs=[VMEM_SPEC, VMEM_SPEC],
        out_specs=VMEM_SPEC,
        compiler_params=KERNEL_PARAMS,
        name="add_shards",
    )(partials, residual.reshape(rows, model_width))
    all_mixed = lax.all_to_all(mixed, "tp", 0, 0)
    next_qkv, new_residual = pl.pallas_call(
        project_kernel,
        out_shape=(
            jax.ShapeDtypeStruct((step_count, 3, row_count, lane_count), jnp.bfloat16),
            jax.ShapeDtypeStruct((rows, model_width), jnp.bfloat16),
        ),
        in_specs=[VMEM_SPEC] * 3,
        out_specs=(VMEM_SPEC, VMEM_SPEC),
        compiler_params=KERNEL_PARAMS,
        name="project",
    )(
        all_mixed,
        norm_gain.reshape(1, model_width),
        qkv_weight.transpose(1, 0, 2),
    )
    return (
        next_qkv.transpose(0, 2, 1, 3),
        new_residual.reshape(step_count, row_count, model_width),
    )


def solution(mesh):
    placed = (
        P(None, "req", "tp"),
        P(None, "req", None, "tp"),
        P(None, "req", None),
        P("req", None, None, "tp"),
        P("req", None, None, "tp"),
        P("req", None),
        P("req"),
        P(None, "req"),
        P("req"),
        P("req"),
        P("req"),
        P("tp", None),
        P(),
        P(None, None, "tp"),
    )
    return jax.shard_map(
        shards,
        mesh=mesh,
        in_specs=placed,
        out_specs=(P(None, "req", None, "tp"), P(None, "req", None)),
        check_vma=False,
    )
```

```python
import math

import jax
import jax.numpy as jnp
from jax import lax
from jax.experimental import pallas as pl
from jax.experimental.pallas import tpu as pltpu
from jax.sharding import PartitionSpec as P

HEAD_DIM = 64
BEAMS = 8

NEG_FILL = -1e30
NORM_EPS = 1e-05
SCORE_SCALE = 1.0 / math.sqrt(HEAD_DIM)
LANES = 2 * HEAD_DIM
STAT_ROWS = 8
NOTE_ROWS = 16


def split_heads(rows):
    lane = lax.broadcasted_iota(jnp.int32, rows.shape, 1)
    zero = jnp.zeros_like(rows)
    return jnp.concatenate(
        [jnp.where(lane < HEAD_DIM, rows, zero), jnp.where(lane >= HEAD_DIM, rows, zero)], axis=0
    )


def join_heads(rows):
    half = rows.shape[0] // 2
    lane = lax.broadcasted_iota(jnp.int32, (half, rows.shape[1]), 1)
    return jnp.where(lane < HEAD_DIM, rows[:half], rows[half:])


def dot_rows(left, right):
    return lax.dot_general(
        left, right, (((1,), (1,)), ((), ())), preferred_element_type=jnp.float32
    )


def to_value_rows(weights):
    return pltpu.roll(weights, 1, axis=1).astype(jnp.bfloat16)


def fill_kernel(query_ref, out_ref, sems):
    copies = [
        pltpu.make_async_copy(query_ref, out_ref.at[index], sems.at[index])
        for index in range(out_ref.shape[0])
    ]
    for copy in copies:
        copy.start()
    for copy in copies:
        copy.wait()


def prompt_kernel(asked_ref, slots_ref, out_ref):
    core = lax.axis_index("req") % 2
    rows = asked_ref.shape[1]
    tokens = slots_ref.shape[1] - NOTE_ROWS
    lane = lax.broadcasted_iota(jnp.int32, (NOTE_ROWS, LANES), 1)
    row = lax.broadcasted_iota(jnp.int32, (NOTE_ROWS, LANES), 0)
    for slot in range(2):
        note = slots_ref[slot, tokens:].astype(jnp.float32)

        def number(index):
            here = jnp.logical_and(row == 0, lane == index)
            return jnp.sum(jnp.where(here, note, 0.0)).astype(jnp.int32)

        owner = number(0)
        live = number(1) * 16 + number(2)

        @pl.when(owner % 2 == core)
        def _():
            chip = owner // 2
            out_ref[chip] = prompt_packet(asked_ref[chip], slots_ref[slot, :tokens], live, rows)


def prompt_packet(query_rows, cache, live, rows):
    queries = split_heads(query_rows)
    scores = dot_rows(queries, cache) * SCORE_SCALE
    column = lax.broadcasted_iota(jnp.int32, scores.shape, 1)
    valid = jnp.logical_and(column % 2 == 0, column < 2 * live)
    scores = jnp.where(valid, scores, NEG_FILL)
    top = jnp.max(scores, axis=1, keepdims=True)
    weights = jnp.exp(scores - top).astype(jnp.bfloat16).astype(jnp.float32)
    total = jnp.sum(weights, axis=1, keepdims=True)
    numer = jnp.dot(to_value_rows(weights), cache, preferred_element_type=jnp.float32)
    mean = join_heads(numer / total).astype(jnp.bfloat16)
    level = top + jnp.log(total)
    high = level.astype(jnp.bfloat16).astype(jnp.float32)
    rest = level - high
    middle = rest.astype(jnp.bfloat16).astype(jnp.float32)
    low = rest - middle
    wide = (2 * rows, LANES)
    lane = lax.broadcasted_iota(jnp.int32, wide, 1)
    row = lax.broadcasted_iota(jnp.int32, wide, 0)
    on_row = lane % HEAD_DIM == row
    first = jnp.sum(
        jnp.where(on_row, jnp.where(lane < HEAD_DIM, high, middle), 0.0), axis=0, keepdims=True
    )
    second = jnp.sum(jnp.where(on_row, low, 0.0), axis=0, keepdims=True)
    stat_row = lax.broadcasted_iota(jnp.int32, (STAT_ROWS, LANES), 0)
    stats = jnp.where(stat_row == 0, first, jnp.where(stat_row == 1, second, 0.0))
    return jnp.concatenate([mean.astype(jnp.float32), stats], axis=0).astype(jnp.bfloat16)


def home_kernel(
    owned_ref,
    live_ref,
    place_ref,
    table_ref,
    length_ref,
    parent_ref,
    query_ref,
    home_ref,
    fresh_ref,
    prompt_ref,
    gain_ref,
    mean_ref,
    level_ref,
    gain_row_ref,
    slot_ref,
    root_ref,
    line_ref,
    note_ref,
    sems,
):
    tokens = prompt_ref.shape[0]
    note_lane = lax.broadcasted_iota(jnp.int32, (NOTE_ROWS, LANES), 1)
    live = live_ref[0]
    note = jnp.where(
        note_lane == 0, owned_ref[0], jnp.where(note_lane == 1, live // 16, live % 16)
    )
    note_ref[...] = note.astype(jnp.float32).astype(jnp.bfloat16)
    copies = [
        pltpu.make_async_copy(prompt_ref, slot_ref.at[pl.ds(0, tokens)], sems.at[0]),
        pltpu.make_async_copy(note_ref, slot_ref.at[pl.ds(tokens, NOTE_ROWS)], sems.at[1]),
    ]
    for copy in copies:
        copy.start()
    step_count = parent_ref.shape[0]
    block_count = table_ref.shape[0]
    rows = query_ref.shape[0]
    block_tokens = home_ref.shape[0] // (2 * block_count)
    unit = (BEAMS, LANES)
    beam_row = lax.broadcasted_iota(jnp.int32, unit, 0)
    lane = lax.broadcasted_iota(jnp.int32, unit, 1)
    is_key = lane % 2 == 0
    half_lane = lane // 2

    def column_of(values):
        built = jnp.full(unit, values[0], jnp.int32)
        for beam in range(1, BEAMS):
            built = jnp.where(beam_row == beam, values[beam], built)
        return built

    counts = []
    fresh_masks = []
    for step in range(step_count):
        roots = []
        for beam in range(BEAMS):
            parent = parent_ref[step, beam]
            root = parent if step == 0 else root_ref[step - 1, parent]
            root_ref[step, beam] = root
            roots.append(root)
            line_ref[step * step_count + step, beam] = beam
            for source in range(step):
                line_ref[step * step_count + source, beam] = line_ref[
                    (step - 1) * step_count + source, parent
                ]
        length = column_of([length_ref[root] for root in roots])
        entries = [
            column_of([table_ref[entry, root] for root in roots]) for entry in range(block_count)
        ]
        pieces = []
        for block in range(block_count):
            limits = [
                jnp.where(entries[entry] == block, length - entry * block_tokens, 0)
                for entry in range(block_count)
            ]
            for part in range(2 * block_tokens // LANES):
                offset = half_lane + part * (LANES // 2)
                count = jnp.zeros(unit, jnp.float32)
                for limit in limits:
                    count = count + jnp.where(offset < limit, 1.0, 0.0)
                pieces.append(jnp.where(is_key, count, 0.0))
        counts.append(jnp.concatenate(pieces, axis=1))
        seen = jnp.zeros(unit, jnp.float32)
        for source in range(step + 1):
            if source == step:
                target = beam_row + source * BEAMS
            else:
                target = (
                    column_of([line_ref[step * step_count + source, beam] for beam in range(BEAMS)])
                    + source * BEAMS
                )
            seen = jnp.where(half_lane == target, 1.0, seen)
        fresh_masks.append(jnp.where(is_key, seen, 0.0))
    count = jnp.concatenate(counts * 2, axis=0)
    fresh_mask = jnp.concatenate(fresh_masks * 2, axis=0)

    queries = split_heads(query_ref[...])
    home = home_ref[...]
    fresh = fresh_ref[...]
    fresh = jnp.concatenate(
        [fresh, jnp.zeros((LANES - fresh.shape[0], LANES), fresh.dtype)], axis=0
    )
    scores = jnp.where(count > 0.0, dot_rows(queries, home) * SCORE_SCALE, NEG_FILL)
    fresh_scores = jnp.where(fresh_mask > 0.0, dot_rows(queries, fresh) * SCORE_SCALE, NEG_FILL)
    top = jnp.maximum(
        jnp.max(scores, axis=1, keepdims=True), jnp.max(fresh_scores, axis=1, keepdims=True)
    )
    weights = jnp.exp(scores - top).astype(jnp.bfloat16).astype(jnp.float32) * count
    weights = weights.astype(jnp.bfloat16).astype(jnp.float32)
    fresh_weights = jnp.exp(fresh_scores - top).astype(jnp.bfloat16).astype(jnp.float32)
    total = jnp.sum(weights, axis=1, keepdims=True) + jnp.sum(fresh_weights, axis=1, keepdims=True)
    numer = jnp.dot(to_value_rows(weights), home, preferred_element_type=jnp.float32)
    numer = numer + jnp.dot(
        to_value_rows(fresh_weights), fresh, preferred_element_type=jnp.float32
    )

    mean_ref[...] = join_heads(numer / total)
    level = jnp.broadcast_to(top + jnp.log(total), numer.shape)
    level_ref[:rows] = join_heads(level)
    level_ref[rows:] = jnp.full((BEAMS, LANES), place_ref[0]).astype(jnp.float32)
    gain_row_ref[...] = gain_ref[...].astype(jnp.float32)
    for copy in copies:
        copy.wait()


def combine_kernel(mean_ref, level_ref, result_ref, weight_ref, out_ref):
    rows = mean_ref.shape[0]
    place = jnp.max(level_ref[rows:]).astype(jnp.int32)
    packet = result_ref[place // 2].astype(jnp.float32)
    wide = (2 * rows, LANES)
    lane = lax.broadcasted_iota(jnp.int32, wide, 1)
    row = lax.broadcasted_iota(jnp.int32, wide, 0)
    on_row = lane % HEAD_DIM == row
    terms = jnp.broadcast_to(packet[rows : rows + 1], wide) + jnp.where(
        lane < HEAD_DIM, jnp.broadcast_to(packet[rows + 1 : rows + 2], wide), 0.0
    )
    prompt_level = jnp.sum(jnp.where(on_row, terms, 0.0), axis=1, keepdims=True)
    prompt_level = join_heads(jnp.broadcast_to(prompt_level, wide))
    level = level_ref[:rows]
    joint_top = jnp.maximum(level, prompt_level)
    home_factor = jnp.exp(level - joint_top)
    prompt_factor = jnp.exp(prompt_level - joint_top)
    attended = (mean_ref[...] * home_factor + packet[:rows] * prompt_factor) / (
        home_factor + prompt_factor
    )
    partial = jnp.dot(
        attended.astype(jnp.bfloat16), weight_ref[...], preferred_element_type=jnp.float32
    )
    width = out_ref.shape[2]
    for index in range(out_ref.shape[0]):
        out_ref[index] = partial[:, index * width : (index + 1) * width].astype(out_ref.dtype)


def sum_kernel(partial_ref, residual_ref, out_ref):
    width = partial_ref.shape[2]
    first = pl.multiple_of(lax.axis_index("tp") * width, width)
    mixed = residual_ref[:, pl.ds(first, width)].astype(jnp.float32)
    for index in range(partial_ref.shape[0]):
        mixed = mixed + partial_ref[index].astype(jnp.float32)
    mixed = mixed.astype(jnp.bfloat16)
    for index in range(out_ref.shape[0]):
        out_ref[index] = mixed


def project_kernel(mixed_ref, gain_ref, qkv_weight_ref, qkv_ref, residual_out_ref):
    shard_count = mixed_ref.shape[0]
    rounded = jnp.concatenate([mixed_ref[index] for index in range(shard_count)], axis=1)
    residual_out_ref[...] = rounded
    mixed = rounded.astype(jnp.float32)
    mean_square = jnp.mean(mixed * mixed, axis=1, keepdims=True)
    normed = (mixed * lax.rsqrt(mean_square + NORM_EPS) * gain_ref[...]).astype(jnp.bfloat16)
    for kind in range(qkv_weight_ref.shape[0]):
        projected = jnp.dot(
            normed, qkv_weight_ref[kind], preferred_element_type=jnp.float32
        ).astype(jnp.bfloat16)
        for step in range(qkv_ref.shape[0]):
            qkv_ref[step, kind] = projected[step * BEAMS : (step + 1) * BEAMS]


VMEM_SPEC = pl.BlockSpec(memory_space=pltpu.VMEM)
SMEM_SPEC = pl.BlockSpec(memory_space=pltpu.SMEM)
KERNEL_PARAMS = pltpu.CompilerParams(vmem_limit_bytes=20 * 1024 * 1024)
ANY_SPEC = pl.BlockSpec(memory_space=pl.ANY)


def shards(
    queries,
    new_kv,
    residual,
    home_cache,
    prompt_cache,
    home_table,
    home_len,
    parents,
    prompt_place,
    owned_request,
    prompt_len,
    out_weight,
    norm_gain,
    qkv_weight,
):
    step_count, row_count, lane_count = queries.shape
    model_width = residual.shape[-1]
    rows = step_count * row_count
    req_size = lax.axis_size("req")
    tp_size = lax.axis_size("tp")
    chips = req_size // 2
    same_core = [[2 * chip + core for chip in range(chips)] for core in range(2)]
    same_chip = [[2 * chip, 2 * chip + 1] for chip in range(chips)]

    def route(slots):
        return lax.all_to_all(slots, "req", 0, 0, axis_index_groups=same_core)

    query_rows = queries.reshape(rows, lane_count)
    asked = route(
        pl.pallas_call(
            fill_kernel,
            out_shape=jax.ShapeDtypeStruct((chips, rows, lane_count), jnp.bfloat16),
            in_specs=[ANY_SPEC],
            out_specs=ANY_SPEC,
            scratch_shapes=[pltpu.SemaphoreType.DMA((chips,))],
            name="fill_slots",
        )(query_rows)
    )

    home_rows = home_cache.reshape(-1, lane_count)
    fresh_rows = new_kv.reshape(-1, lane_count)
    prompt_rows = prompt_cache.reshape(-1, lane_count)
    slot_rows = prompt_rows.shape[0] + NOTE_ROWS
    home_mean, home_level, gain_row, own_slot = pl.pallas_call(
        home_kernel,
        out_shape=(
            jax.ShapeDtypeStruct((rows, lane_count), jnp.float32),
            jax.ShapeDtypeStruct((rows + BEAMS, lane_count), jnp.float32),
            jax.ShapeDtypeStruct((1, model_width), jnp.float32),
            jax.ShapeDtypeStruct((slot_rows, lane_count), jnp.bfloat16),
        ),
        in_specs=[SMEM_SPEC] * 6 + [VMEM_SPEC] * 3 + [ANY_SPEC, VMEM_SPEC],
        out_specs=(VMEM_SPEC, VMEM_SPEC, VMEM_SPEC, ANY_SPEC),
        scratch_shapes=[
            pltpu.SMEM((step_count, BEAMS), jnp.int32),
            pltpu.SMEM((step_count * step_count, BEAMS), jnp.int32),
            pltpu.VMEM((NOTE_ROWS, lane_count), jnp.bfloat16),
            pltpu.SemaphoreType.DMA((2,)),
        ],
        name="home_attention",
    )(
        owned_request,
        prompt_len,
        prompt_place,
        home_table.T,
        home_len,
        parents,
        query_rows,
        home_rows,
        fresh_rows,
        prompt_rows,
        norm_gain.reshape(1, model_width),
    )
    both_slots = lax.all_gather(own_slot, "req", axis_index_groups=same_chip)

    packet_rows = rows + STAT_ROWS
    results = pl.pallas_call(
        prompt_kernel,
        out_shape=pltpu.VMEM((chips, packet_rows, lane_count), jnp.bfloat16),
        in_specs=[VMEM_SPEC] * 2,
        out_specs=VMEM_SPEC,
        compiler_params=KERNEL_PARAMS,
        name="prompt_attention",
    )(asked, both_slots)
    returned = route(results)

    width = model_width // tp_size
    partial = pl.pallas_call(
        combine_kernel,
        out_shape=jax.ShapeDtypeStruct((tp_size, rows, width), jnp.float32),
        in_specs=[VMEM_SPEC] * 4,
        out_specs=VMEM_SPEC,
        compiler_params=KERNEL_PARAMS,
        name="combine",
    )(home_mean, home_level, returned, out_weight)
    partials = lax.all_to_all(partial, "tp", 0, 0)
    mixed = pl.pallas_call(
        sum_kernel,
        out_shape=jax.ShapeDtypeStruct((tp_size, rows, width), jnp.bfloat16),
        in_specs=[VMEM_SPEC, VMEM_SPEC],
        out_specs=VMEM_SPEC,
        compiler_params=KERNEL_PARAMS,
        name="add_shards",
    )(partials, residual.reshape(rows, model_width))
    all_mixed = lax.all_to_all(mixed, "tp", 0, 0)
    next_qkv, new_residual = pl.pallas_call(
        project_kernel,
        out_shape=(
            jax.ShapeDtypeStruct((step_count, 3, row_count, lane_count), jnp.bfloat16),
            jax.ShapeDtypeStruct((rows, model_width), jnp.bfloat16),
        ),
        in_specs=[VMEM_SPEC] * 3,
        out_specs=(VMEM_SPEC, VMEM_SPEC),
        compiler_params=KERNEL_PARAMS,
        name="project",
    )(
        all_mixed,
        gain_row,
        qkv_weight.transpose(1, 0, 2),
    )
    return (
        next_qkv.transpose(0, 2, 1, 3),
        new_residual.reshape(step_count, row_count, model_width),
    )


def solution(mesh):
    placed = (
        P(None, "req", "tp"),
        P(None, "req", None, "tp"),
        P(None, "req", None),
        P("req", None, None, "tp"),
        P("req", None, None, "tp"),
        P("req", None),
        P("req"),
        P(None, "req"),
        P("req"),
        P("req"),
        P("req"),
        P("tp", None),
        P(),
        P(None, None, "tp"),
    )
    return jax.shard_map(
        shards,
        mesh=mesh,
        in_specs=placed,
        out_specs=(P(None, "req", None, "tp"), P(None, "req", None)),
        check_vma=False,
    )
```

```python
import math

import jax
import jax.numpy as jnp
from jax import lax
from jax.experimental import pallas as pl
from jax.experimental.pallas import tpu as pltpu
from jax.sharding import PartitionSpec as P

HEAD_DIM = 64
BEAMS = 8

NEG_FILL = -1e30
NORM_EPS = 1e-05
SCORE_SCALE = 1.0 / math.sqrt(HEAD_DIM)
LANES = 2 * HEAD_DIM
STAT_ROWS = 8
NOTE_ROWS = 16


def split_heads(rows):
    lane = lax.broadcasted_iota(jnp.int32, rows.shape, 1)
    zero = jnp.zeros_like(rows)
    return jnp.concatenate(
        [jnp.where(lane < HEAD_DIM, rows, zero), jnp.where(lane >= HEAD_DIM, rows, zero)], axis=0
    )


def join_heads(rows):
    half = rows.shape[0] // 2
    lane = lax.broadcasted_iota(jnp.int32, (half, rows.shape[1]), 1)
    return jnp.where(lane < HEAD_DIM, rows[:half], rows[half:])


def dot_rows(left, right):
    return lax.dot_general(
        left, right, (((1,), (1,)), ((), ())), preferred_element_type=jnp.float32
    )


def to_value_rows(weights):
    return pltpu.roll(weights, 1, axis=1).astype(jnp.bfloat16)


def prompt_kernel(asked_ref, slots_ref, out_ref):
    core = lax.axis_index("req") % 2
    rows = asked_ref.shape[1]
    tokens = slots_ref.shape[1] - NOTE_ROWS
    lane = lax.broadcasted_iota(jnp.int32, (NOTE_ROWS, LANES), 1)
    row = lax.broadcasted_iota(jnp.int32, (NOTE_ROWS, LANES), 0)
    for slot in range(2):
        note = slots_ref[slot, tokens:].astype(jnp.float32)

        def number(index):
            here = jnp.logical_and(row == 0, lane == index)
            return jnp.sum(jnp.where(here, note, 0.0)).astype(jnp.int32)

        owner = number(0)
        live = number(1) * 16 + number(2)

        @pl.when(owner % 2 == core)
        def _():
            chip = owner // 2
            out_ref[chip] = prompt_packet(asked_ref[chip], slots_ref[slot, :tokens], live, rows)


def prompt_packet(query_rows, cache, live, rows):
    queries = split_heads(query_rows)
    scores = dot_rows(queries, cache) * SCORE_SCALE
    column = lax.broadcasted_iota(jnp.int32, scores.shape, 1)
    valid = jnp.logical_and(column % 2 == 0, column < 2 * live)
    scores = jnp.where(valid, scores, NEG_FILL)
    top = jnp.max(scores, axis=1, keepdims=True)
    weights = jnp.exp(scores - top).astype(jnp.bfloat16).astype(jnp.float32)
    total = jnp.sum(weights, axis=1, keepdims=True)
    numer = jnp.dot(to_value_rows(weights), cache, preferred_element_type=jnp.float32)
    mean = join_heads(numer / total).astype(jnp.bfloat16)
    level = top + jnp.log(total)
    high = level.astype(jnp.bfloat16).astype(jnp.float32)
    rest = level - high
    middle = rest.astype(jnp.bfloat16).astype(jnp.float32)
    low = rest - middle
    wide = (2 * rows, LANES)
    lane = lax.broadcasted_iota(jnp.int32, wide, 1)
    row = lax.broadcasted_iota(jnp.int32, wide, 0)
    on_row = lane % HEAD_DIM == row
    first = jnp.sum(
        jnp.where(on_row, jnp.where(lane < HEAD_DIM, high, middle), 0.0), axis=0, keepdims=True
    )
    second = jnp.sum(jnp.where(on_row, low, 0.0), axis=0, keepdims=True)
    stat_row = lax.broadcasted_iota(jnp.int32, (STAT_ROWS, LANES), 0)
    stats = jnp.where(stat_row == 0, first, jnp.where(stat_row == 1, second, 0.0))
    return jnp.concatenate([mean.astype(jnp.float32), stats], axis=0).astype(jnp.bfloat16)


def home_kernel(
    owned_ref,
    live_ref,
    place_ref,
    table_ref,
    length_ref,
    parent_ref,
    query_ref,
    home_ref,
    fresh_ref,
    prompt_ref,
    mean_ref,
    level_ref,
    slot_ref,
    root_ref,
    line_ref,
):
    tokens = prompt_ref.shape[0]
    note_lane = lax.broadcasted_iota(jnp.int32, (NOTE_ROWS, LANES), 1)
    live = live_ref[0]
    note = jnp.where(
        note_lane == 0, owned_ref[0], jnp.where(note_lane == 1, live // 16, live % 16)
    )
    slot_ref[:tokens] = prompt_ref[...]
    slot_ref[tokens:] = note.astype(jnp.float32).astype(jnp.bfloat16)
    step_count = parent_ref.shape[0]
    block_count = table_ref.shape[0]
    rows = query_ref.shape[0]
    block_tokens = home_ref.shape[0] // (2 * block_count)
    unit = (BEAMS, LANES)
    beam_row = lax.broadcasted_iota(jnp.int32, unit, 0)
    lane = lax.broadcasted_iota(jnp.int32, unit, 1)
    is_key = lane % 2 == 0
    half_lane = lane // 2

    def column_of(values):
        built = jnp.full(unit, values[0], jnp.int32)
        for beam in range(1, BEAMS):
            built = jnp.where(beam_row == beam, values[beam], built)
        return built

    counts = []
    fresh_masks = []
    for step in range(step_count):
        roots = []
        for beam in range(BEAMS):
            parent = parent_ref[step, beam]
            root = parent if step == 0 else root_ref[step - 1, parent]
            root_ref[step, beam] = root
            roots.append(root)
            line_ref[step * step_count + step, beam] = beam
            for source in range(step):
                line_ref[step * step_count + source, beam] = line_ref[
                    (step - 1) * step_count + source, parent
                ]
        length = column_of([length_ref[root] for root in roots])
        entries = [
            column_of([table_ref[entry, root] for root in roots]) for entry in range(block_count)
        ]
        pieces = []
        for block in range(block_count):
            limits = [
                jnp.where(entries[entry] == block, length - entry * block_tokens, 0)
                for entry in range(block_count)
            ]
            for part in range(2 * block_tokens // LANES):
                offset = half_lane + part * (LANES // 2)
                count = jnp.zeros(unit, jnp.float32)
                for limit in limits:
                    count = count + jnp.where(offset < limit, 1.0, 0.0)
                pieces.append(jnp.where(is_key, count, 0.0))
        counts.append(jnp.concatenate(pieces, axis=1))
        seen = jnp.zeros(unit, jnp.float32)
        for source in range(step + 1):
            if source == step:
                target = beam_row + source * BEAMS
            else:
                target = (
                    column_of([line_ref[step * step_count + source, beam] for beam in range(BEAMS)])
                    + source * BEAMS
                )
            seen = jnp.where(half_lane == target, 1.0, seen)
        fresh_masks.append(jnp.where(is_key, seen, 0.0))
    count = jnp.concatenate(counts * 2, axis=0)
    fresh_mask = jnp.concatenate(fresh_masks * 2, axis=0)

    queries = split_heads(query_ref[...])
    home = home_ref[...]
    fresh = fresh_ref[...]
    fresh = jnp.concatenate(
        [fresh, jnp.zeros((LANES - fresh.shape[0], LANES), fresh.dtype)], axis=0
    )
    scores = jnp.where(count > 0.0, dot_rows(queries, home) * SCORE_SCALE, NEG_FILL)
    fresh_scores = jnp.where(fresh_mask > 0.0, dot_rows(queries, fresh) * SCORE_SCALE, NEG_FILL)
    top = jnp.maximum(
        jnp.max(scores, axis=1, keepdims=True), jnp.max(fresh_scores, axis=1, keepdims=True)
    )
    weights = jnp.exp(scores - top).astype(jnp.bfloat16).astype(jnp.float32) * count
    weights = weights.astype(jnp.bfloat16).astype(jnp.float32)
    fresh_weights = jnp.exp(fresh_scores - top).astype(jnp.bfloat16).astype(jnp.float32)
    total = jnp.sum(weights, axis=1, keepdims=True) + jnp.sum(fresh_weights, axis=1, keepdims=True)
    numer = jnp.dot(to_value_rows(weights), home, preferred_element_type=jnp.float32)
    numer = numer + jnp.dot(
        to_value_rows(fresh_weights), fresh, preferred_element_type=jnp.float32
    )

    mean_ref[...] = join_heads(numer / total)
    level = jnp.broadcast_to(top + jnp.log(total), numer.shape)
    level_ref[:rows] = join_heads(level)
    level_ref[rows:] = jnp.full((BEAMS, LANES), place_ref[0]).astype(jnp.float32)


def combine_kernel(mean_ref, level_ref, result_ref, weight_ref, out_ref):
    rows = mean_ref.shape[0]
    place = jnp.max(level_ref[rows:]).astype(jnp.int32)
    packet = result_ref[place // 2].astype(jnp.float32)
    wide = (2 * rows, LANES)
    lane = lax.broadcasted_iota(jnp.int32, wide, 1)
    row = lax.broadcasted_iota(jnp.int32, wide, 0)
    on_row = lane % HEAD_DIM == row
    terms = jnp.broadcast_to(packet[rows : rows + 1], wide) + jnp.where(
        lane < HEAD_DIM, jnp.broadcast_to(packet[rows + 1 : rows + 2], wide), 0.0
    )
    prompt_level = jnp.sum(jnp.where(on_row, terms, 0.0), axis=1, keepdims=True)
    prompt_level = join_heads(jnp.broadcast_to(prompt_level, wide))
    level = level_ref[:rows]
    joint_top = jnp.maximum(level, prompt_level)
    home_factor = jnp.exp(level - joint_top)
    prompt_factor = jnp.exp(prompt_level - joint_top)
    attended = (mean_ref[...] * home_factor + packet[:rows] * prompt_factor) / (
        home_factor + prompt_factor
    )
    partial = jnp.dot(
        attended.astype(jnp.bfloat16), weight_ref[...], preferred_element_type=jnp.float32
    )
    width = out_ref.shape[2]
    for index in range(out_ref.shape[0]):
        out_ref[index] = partial[:, index * width : (index + 1) * width].astype(out_ref.dtype)


def sum_kernel(partial_ref, residual_ref, out_ref):
    width = partial_ref.shape[2]
    first = pl.multiple_of(lax.axis_index("tp") * width, width)
    mixed = residual_ref[:, pl.ds(first, width)].astype(jnp.float32)
    for index in range(partial_ref.shape[0]):
        mixed = mixed + partial_ref[index].astype(jnp.float32)
    mixed = mixed.astype(jnp.bfloat16)
    for index in range(out_ref.shape[0]):
        out_ref[index] = mixed


def project_kernel(mixed_ref, gain_ref, qkv_weight_ref, qkv_ref, residual_out_ref):
    shard_count = mixed_ref.shape[0]
    rounded = jnp.concatenate([mixed_ref[index] for index in range(shard_count)], axis=1)
    residual_out_ref[...] = rounded
    mixed = rounded.astype(jnp.float32)
    mean_square = jnp.mean(mixed * mixed, axis=1, keepdims=True)
    gain_rows = gain_ref[...].astype(jnp.float32)
    gain = jnp.concatenate(
        [gain_rows[index : index + 1] for index in range(gain_rows.shape[0])], axis=1
    )
    normed = (mixed * lax.rsqrt(mean_square + NORM_EPS) * gain).astype(jnp.bfloat16)
    for kind in range(qkv_weight_ref.shape[0]):
        projected = jnp.dot(
            normed, qkv_weight_ref[kind], preferred_element_type=jnp.float32
        ).astype(jnp.bfloat16)
        for step in range(qkv_ref.shape[0]):
            qkv_ref[step, kind] = projected[step * BEAMS : (step + 1) * BEAMS]


VMEM_SPEC = pl.BlockSpec(memory_space=pltpu.VMEM)
SMEM_SPEC = pl.BlockSpec(memory_space=pltpu.SMEM)
KERNEL_PARAMS = pltpu.CompilerParams(vmem_limit_bytes=20 * 1024 * 1024)


def shards(
    queries,
    new_kv,
    residual,
    home_cache,
    prompt_cache,
    home_table,
    home_len,
    parents,
    prompt_place,
    owned_request,
    prompt_len,
    out_weight,
    norm_gain,
    qkv_weight,
):
    step_count, row_count, lane_count = queries.shape
    model_width = residual.shape[-1]
    rows = step_count * row_count
    req_size = lax.axis_size("req")
    tp_size = lax.axis_size("tp")
    chips = req_size // 2
    same_core = [[2 * chip + core for chip in range(chips)] for core in range(2)]
    same_chip = [[2 * chip, 2 * chip + 1] for chip in range(chips)]

    def route(slots):
        return lax.all_to_all(slots, "req", 0, 0, axis_index_groups=same_core)

    query_rows = queries.reshape(rows, lane_count)
    asked = route(jnp.broadcast_to(query_rows[None], (chips, rows, lane_count)))

    home_rows = home_cache.reshape(-1, lane_count)
    fresh_rows = new_kv.reshape(-1, lane_count)
    prompt_rows = prompt_cache.reshape(-1, lane_count)
    slot_rows = prompt_rows.shape[0] + NOTE_ROWS
    home_mean, home_level, own_slot = pl.pallas_call(
        home_kernel,
        out_shape=(
            jax.ShapeDtypeStruct((rows, lane_count), jnp.float32),
            jax.ShapeDtypeStruct((rows + BEAMS, lane_count), jnp.float32),
            jax.ShapeDtypeStruct((slot_rows, lane_count), jnp.bfloat16),
        ),
        in_specs=[SMEM_SPEC] * 6 + [VMEM_SPEC] * 4,
        out_specs=(VMEM_SPEC, VMEM_SPEC, VMEM_SPEC),
        scratch_shapes=[
            pltpu.SMEM((step_count, BEAMS), jnp.int32),
            pltpu.SMEM((step_count * step_count, BEAMS), jnp.int32),
        ],
        name="home_attention",
    )(
        owned_request,
        prompt_len,
        prompt_place,
        home_table.T,
        home_len,
        parents,
        query_rows,
        home_rows,
        fresh_rows,
        prompt_rows,
    )
    both_slots = lax.all_gather(own_slot, "req", axis_index_groups=same_chip)

    packet_rows = rows + STAT_ROWS
    results = pl.pallas_call(
        prompt_kernel,
        out_shape=pltpu.VMEM((chips, packet_rows, lane_count), jnp.bfloat16),
        in_specs=[VMEM_SPEC] * 2,
        out_specs=VMEM_SPEC,
        compiler_params=KERNEL_PARAMS,
        name="prompt_attention",
    )(asked, both_slots)
    returned = route(results)

    width = model_width // tp_size
    partial = pl.pallas_call(
        combine_kernel,
        out_shape=jax.ShapeDtypeStruct((tp_size, rows, width), jnp.bfloat16),
        in_specs=[VMEM_SPEC] * 4,
        out_specs=VMEM_SPEC,
        compiler_params=KERNEL_PARAMS,
        name="combine",
    )(home_mean, home_level, returned, out_weight)
    partials = lax.all_to_all(partial, "tp", 0, 0)
    mixed = pl.pallas_call(
        sum_kernel,
        out_shape=jax.ShapeDtypeStruct((tp_size, rows, width), jnp.bfloat16),
        in_specs=[VMEM_SPEC, VMEM_SPEC],
        out_specs=VMEM_SPEC,
        compiler_params=KERNEL_PARAMS,
        name="add_shards",
    )(partials, residual.reshape(rows, model_width))
    all_mixed = lax.all_to_all(mixed, "tp", 0, 0)
    next_qkv, new_residual = pl.pallas_call(
        project_kernel,
        out_shape=(
            jax.ShapeDtypeStruct((step_count, 3, row_count, lane_count), jnp.bfloat16),
            jax.ShapeDtypeStruct((rows, model_width), jnp.bfloat16),
        ),
        in_specs=[VMEM_SPEC] * 3,
        out_specs=(VMEM_SPEC, VMEM_SPEC),
        compiler_params=KERNEL_PARAMS,
        name="project",
    )(
        all_mixed,
        norm_gain.reshape(model_width // lane_count, lane_count),
        qkv_weight.transpose(1, 0, 2),
    )
    return (
        next_qkv.transpose(0, 2, 1, 3),
        new_residual.reshape(step_count, row_count, model_width),
    )


def solution(mesh):
    placed = (
        P(None, "req", "tp"),
        P(None, "req", None, "tp"),
        P(None, "req", None),
        P("req", None, None, "tp"),
        P("req", None, None, "tp"),
        P("req", None),
        P("req"),
        P(None, "req"),
        P("req"),
        P("req"),
        P("req"),
        P("tp", None),
        P(),
        P(None, None, "tp"),
    )
    return jax.shard_map(
        shards,
        mesh=mesh,
        in_specs=placed,
        out_specs=(P(None, "req", None, "tp"), P(None, "req", None)),
        check_vma=False,
    )
```

```python
import math

import jax
import jax.numpy as jnp
from jax import lax
from jax.experimental import pallas as pl
from jax.experimental.pallas import tpu as pltpu
from jax.sharding import PartitionSpec as P

HEAD_DIM = 64
BEAMS = 8

NEG_FILL = -1e30
NORM_EPS = 1e-05
SCORE_SCALE = 1.0 / math.sqrt(HEAD_DIM)
LANES = 2 * HEAD_DIM
STAT_ROWS = 8
NOTE_ROWS = 16


def split_heads(rows):
    lane = lax.broadcasted_iota(jnp.int32, rows.shape, 1)
    zero = jnp.zeros_like(rows)
    return jnp.concatenate(
        [jnp.where(lane < HEAD_DIM, rows, zero), jnp.where(lane >= HEAD_DIM, rows, zero)], axis=0
    )


def join_heads(rows):
    half = rows.shape[0] // 2
    lane = lax.broadcasted_iota(jnp.int32, (half, rows.shape[1]), 1)
    return jnp.where(lane < HEAD_DIM, rows[:half], rows[half:])


def dot_rows(left, right):
    return lax.dot_general(
        left, right, (((1,), (1,)), ((), ())), preferred_element_type=jnp.float32
    )


def to_value_rows(weights):
    return pltpu.roll(weights, 1, axis=1).astype(jnp.bfloat16)


def fill_kernel(query_ref, out_ref):
    for index in range(out_ref.shape[0]):
        out_ref[index] = query_ref[...]


def prompt_kernel(asked_ref, slots_ref, out_ref):
    core = lax.axis_index("req") % 2
    rows = asked_ref.shape[1]
    tokens = slots_ref.shape[1] - NOTE_ROWS
    lane = lax.broadcasted_iota(jnp.int32, (NOTE_ROWS, LANES), 1)
    row = lax.broadcasted_iota(jnp.int32, (NOTE_ROWS, LANES), 0)
    served = []
    for slot in range(2):
        note = slots_ref[slot, tokens:].astype(jnp.float32)

        def number(index):
            here = jnp.logical_and(row == 0, lane == index)
            return jnp.sum(jnp.where(here, note, 0.0)).astype(jnp.int32)

        owner = number(0)
        live = number(1) * 16 + number(2)
        served.append(
            (owner, prompt_packet(asked_ref[owner // 2], slots_ref[slot, :tokens], live, rows))
        )
    for owner, packet in served:

        @pl.when(owner % 2 == core)
        def _():
            out_ref[owner // 2] = packet


def prompt_packet(query_rows, cache, live, rows):
    queries = split_heads(query_rows)
    scores = dot_rows(queries, cache) * SCORE_SCALE
    column = lax.broadcasted_iota(jnp.int32, scores.shape, 1)
    valid = jnp.logical_and(column % 2 == 0, column < 2 * live)
    scores = jnp.where(valid, scores, NEG_FILL)
    top = jnp.max(scores, axis=1, keepdims=True)
    weights = jnp.exp(scores - top).astype(jnp.bfloat16).astype(jnp.float32)
    total = jnp.sum(weights, axis=1, keepdims=True)
    numer = jnp.dot(to_value_rows(weights), cache, preferred_element_type=jnp.float32)
    mean = join_heads(numer / total).astype(jnp.bfloat16)
    level = top + jnp.log(total)
    high = level.astype(jnp.bfloat16).astype(jnp.float32)
    rest = level - high
    middle = rest.astype(jnp.bfloat16).astype(jnp.float32)
    low = rest - middle
    wide = (2 * rows, LANES)
    lane = lax.broadcasted_iota(jnp.int32, wide, 1)
    row = lax.broadcasted_iota(jnp.int32, wide, 0)
    on_row = lane % HEAD_DIM == row
    first = jnp.sum(
        jnp.where(on_row, jnp.where(lane < HEAD_DIM, high, middle), 0.0), axis=0, keepdims=True
    )
    second = jnp.sum(jnp.where(on_row, low, 0.0), axis=0, keepdims=True)
    stat_row = lax.broadcasted_iota(jnp.int32, (STAT_ROWS, LANES), 0)
    stats = jnp.where(stat_row == 0, first, jnp.where(stat_row == 1, second, 0.0))
    return jnp.concatenate([mean.astype(jnp.float32), stats], axis=0).astype(jnp.bfloat16)


def home_kernel(
    owned_ref,
    live_ref,
    place_ref,
    table_ref,
    length_ref,
    parent_ref,
    query_ref,
    home_ref,
    fresh_ref,
    prompt_ref,
    mean_ref,
    level_ref,
    slot_ref,
    root_ref,
    line_ref,
):
    tokens = prompt_ref.shape[0]
    note_lane = lax.broadcasted_iota(jnp.int32, (NOTE_ROWS, LANES), 1)
    live = live_ref[0]
    note = jnp.where(
        note_lane == 0, owned_ref[0], jnp.where(note_lane == 1, live // 16, live % 16)
    )
    slot_ref[:tokens] = prompt_ref[...]
    slot_ref[tokens:] = note.astype(jnp.float32).astype(jnp.bfloat16)
    step_count = parent_ref.shape[0]
    block_count = table_ref.shape[0]
    rows = query_ref.shape[0]
    block_tokens = home_ref.shape[0] // (2 * block_count)
    unit = (BEAMS, LANES)
    beam_row = lax.broadcasted_iota(jnp.int32, unit, 0)
    lane = lax.broadcasted_iota(jnp.int32, unit, 1)
    is_key = lane % 2 == 0
    half_lane = lane // 2

    def column_of(values):
        built = jnp.full(unit, values[0], jnp.int32)
        for beam in range(1, BEAMS):
            built = jnp.where(beam_row == beam, values[beam], built)
        return built

    counts = []
    fresh_masks = []
    for step in range(step_count):
        roots = []
        for beam in range(BEAMS):
            parent = parent_ref[step, beam]
            root = parent if step == 0 else root_ref[step - 1, parent]
            root_ref[step, beam] = root
            roots.append(root)
            line_ref[step * step_count + step, beam] = beam
            for source in range(step):
                line_ref[step * step_count + source, beam] = line_ref[
                    (step - 1) * step_count + source, parent
                ]
        length = column_of([length_ref[root] for root in roots])
        entries = [
            column_of([table_ref[entry, root] for root in roots]) for entry in range(block_count)
        ]
        pieces = []
        for block in range(block_count):
            limits = [
                jnp.where(entries[entry] == block, length - entry * block_tokens, 0)
                for entry in range(block_count)
            ]
            for part in range(2 * block_tokens // LANES):
                offset = half_lane + part * (LANES // 2)
                count = jnp.zeros(unit, jnp.float32)
                for limit in limits:
                    count = count + jnp.where(offset < limit, 1.0, 0.0)
                pieces.append(jnp.where(is_key, count, 0.0))
        counts.append(jnp.concatenate(pieces, axis=1))
        seen = jnp.zeros(unit, jnp.float32)
        for source in range(step + 1):
            if source == step:
                target = beam_row + source * BEAMS
            else:
                target = (
                    column_of([line_ref[step * step_count + source, beam] for beam in range(BEAMS)])
                    + source * BEAMS
                )
            seen = jnp.where(half_lane == target, 1.0, seen)
        fresh_masks.append(jnp.where(is_key, seen, 0.0))
    count = jnp.concatenate(counts * 2, axis=0)
    fresh_mask = jnp.concatenate(fresh_masks * 2, axis=0)

    queries = split_heads(query_ref[...])
    home = home_ref[...]
    fresh = fresh_ref[...]
    fresh = jnp.concatenate(
        [fresh, jnp.zeros((LANES - fresh.shape[0], LANES), fresh.dtype)], axis=0
    )
    scores = jnp.where(count > 0.0, dot_rows(queries, home) * SCORE_SCALE, NEG_FILL)
    fresh_scores = jnp.where(fresh_mask > 0.0, dot_rows(queries, fresh) * SCORE_SCALE, NEG_FILL)
    top = jnp.maximum(
        jnp.max(scores, axis=1, keepdims=True), jnp.max(fresh_scores, axis=1, keepdims=True)
    )
    weights = jnp.exp(scores - top).astype(jnp.bfloat16).astype(jnp.float32) * count
    weights = weights.astype(jnp.bfloat16).astype(jnp.float32)
    fresh_weights = jnp.exp(fresh_scores - top).astype(jnp.bfloat16).astype(jnp.float32)
    total = jnp.sum(weights, axis=1, keepdims=True) + jnp.sum(fresh_weights, axis=1, keepdims=True)
    numer = jnp.dot(to_value_rows(weights), home, preferred_element_type=jnp.float32)
    numer = numer + jnp.dot(
        to_value_rows(fresh_weights), fresh, preferred_element_type=jnp.float32
    )

    mean_ref[...] = join_heads(numer / total)
    level = jnp.broadcast_to(top + jnp.log(total), numer.shape)
    level_ref[:rows] = join_heads(level)
    level_ref[rows:] = jnp.full((BEAMS, LANES), place_ref[0]).astype(jnp.float32)


def combine_kernel(mean_ref, level_ref, result_ref, weight_ref, out_ref):
    rows = mean_ref.shape[0]
    place = jnp.max(level_ref[rows:]).astype(jnp.int32)
    packet = result_ref[place // 2].astype(jnp.float32)
    wide = (2 * rows, LANES)
    lane = lax.broadcasted_iota(jnp.int32, wide, 1)
    row = lax.broadcasted_iota(jnp.int32, wide, 0)
    on_row = lane % HEAD_DIM == row
    terms = jnp.broadcast_to(packet[rows : rows + 1], wide) + jnp.where(
        lane < HEAD_DIM, jnp.broadcast_to(packet[rows + 1 : rows + 2], wide), 0.0
    )
    prompt_level = jnp.sum(jnp.where(on_row, terms, 0.0), axis=1, keepdims=True)
    prompt_level = join_heads(jnp.broadcast_to(prompt_level, wide))
    level = level_ref[:rows]
    joint_top = jnp.maximum(level, prompt_level)
    home_factor = jnp.exp(level - joint_top)
    prompt_factor = jnp.exp(prompt_level - joint_top)
    attended = (mean_ref[...] * home_factor + packet[:rows] * prompt_factor) / (
        home_factor + prompt_factor
    )
    partial = jnp.dot(
        attended.astype(jnp.bfloat16), weight_ref[...], preferred_element_type=jnp.float32
    )
    width = out_ref.shape[2]
    for index in range(out_ref.shape[0]):
        out_ref[index] = partial[:, index * width : (index + 1) * width].astype(out_ref.dtype)


def sum_kernel(partial_ref, residual_ref, out_ref):
    width = partial_ref.shape[2]
    first = pl.multiple_of(lax.axis_index("tp") * width, width)
    mixed = residual_ref[:, pl.ds(first, width)].astype(jnp.float32)
    for index in range(partial_ref.shape[0]):
        mixed = mixed + partial_ref[index].astype(jnp.float32)
    mixed = mixed.astype(jnp.bfloat16)
    for index in range(out_ref.shape[0]):
        out_ref[index] = mixed


def project_kernel(mixed_ref, gain_ref, qkv_weight_ref, qkv_ref, residual_out_ref):
    shard_count = mixed_ref.shape[0]
    rounded = jnp.concatenate([mixed_ref[index] for index in range(shard_count)], axis=1)
    residual_out_ref[...] = rounded
    mixed = rounded.astype(jnp.float32)
    mean_square = jnp.mean(mixed * mixed, axis=1, keepdims=True)
    gain_rows = gain_ref[...].astype(jnp.float32)
    gain = jnp.concatenate(
        [gain_rows[index : index + 1] for index in range(gain_rows.shape[0])], axis=1
    )
    normed = (mixed * lax.rsqrt(mean_square + NORM_EPS) * gain).astype(jnp.bfloat16)
    for kind in range(qkv_weight_ref.shape[0]):
        projected = jnp.dot(
            normed, qkv_weight_ref[kind], preferred_element_type=jnp.float32
        ).astype(jnp.bfloat16)
        for step in range(qkv_ref.shape[0]):
            qkv_ref[step, kind] = projected[step * BEAMS : (step + 1) * BEAMS]


VMEM_SPEC = pl.BlockSpec(memory_space=pltpu.VMEM)
SMEM_SPEC = pl.BlockSpec(memory_space=pltpu.SMEM)
KERNEL_PARAMS = pltpu.CompilerParams(vmem_limit_bytes=20 * 1024 * 1024)


def shards(
    queries,
    new_kv,
    residual,
    home_cache,
    prompt_cache,
    home_table,
    home_len,
    parents,
    prompt_place,
    owned_request,
    prompt_len,
    out_weight,
    norm_gain,
    qkv_weight,
):
    step_count, row_count, lane_count = queries.shape
    model_width = residual.shape[-1]
    rows = step_count * row_count
    req_size = lax.axis_size("req")
    tp_size = lax.axis_size("tp")
    chips = req_size // 2
    same_core = [[2 * chip + core for chip in range(chips)] for core in range(2)]
    same_chip = [[2 * chip, 2 * chip + 1] for chip in range(chips)]

    def route(slots):
        return lax.all_to_all(slots, "req", 0, 0, axis_index_groups=same_core)

    query_rows = queries.reshape(rows, lane_count)
    asked = route(
        pl.pallas_call(
            fill_kernel,
            out_shape=jax.ShapeDtypeStruct((chips, rows, lane_count), jnp.bfloat16),
            in_specs=[VMEM_SPEC],
            out_specs=VMEM_SPEC,
            name="fill_slots",
        )(query_rows)
    )

    home_rows = home_cache.reshape(-1, lane_count)
    fresh_rows = new_kv.reshape(-1, lane_count)
    prompt_rows = prompt_cache.reshape(-1, lane_count)
    slot_rows = prompt_rows.shape[0] + NOTE_ROWS
    home_mean, home_level, own_slot = pl.pallas_call(
        home_kernel,
        out_shape=(
            jax.ShapeDtypeStruct((rows, lane_count), jnp.float32),
            jax.ShapeDtypeStruct((rows + BEAMS, lane_count), jnp.float32),
            jax.ShapeDtypeStruct((slot_rows, lane_count), jnp.bfloat16),
        ),
        in_specs=[SMEM_SPEC] * 6 + [VMEM_SPEC] * 4,
        out_specs=(VMEM_SPEC, VMEM_SPEC, VMEM_SPEC),
        scratch_shapes=[
            pltpu.SMEM((step_count, BEAMS), jnp.int32),
            pltpu.SMEM((step_count * step_count, BEAMS), jnp.int32),
        ],
        name="home_attention",
    )(
        owned_request,
        prompt_len,
        prompt_place,
        home_table.T,
        home_len,
        parents,
        query_rows,
        home_rows,
        fresh_rows,
        prompt_rows,
    )
    both_slots = lax.all_gather(own_slot, "req", axis_index_groups=same_chip)

    packet_rows = rows + STAT_ROWS
    results = pl.pallas_call(
        prompt_kernel,
        out_shape=pltpu.VMEM((chips, packet_rows, lane_count), jnp.bfloat16),
        in_specs=[VMEM_SPEC] * 2,
        out_specs=VMEM_SPEC,
        compiler_params=KERNEL_PARAMS,
        name="prompt_attention",
    )(asked, both_slots)
    returned = route(results)

    width = model_width // tp_size
    partial = pl.pallas_call(
        combine_kernel,
        out_shape=jax.ShapeDtypeStruct((tp_size, rows, width), jnp.bfloat16),
        in_specs=[VMEM_SPEC] * 4,
        out_specs=VMEM_SPEC,
        compiler_params=KERNEL_PARAMS,
        name="combine",
    )(home_mean, home_level, returned, out_weight)
    partials = lax.all_to_all(partial, "tp", 0, 0)
    mixed = pl.pallas_call(
        sum_kernel,
        out_shape=jax.ShapeDtypeStruct((tp_size, rows, width), jnp.bfloat16),
        in_specs=[VMEM_SPEC, VMEM_SPEC],
        out_specs=VMEM_SPEC,
        compiler_params=KERNEL_PARAMS,
        name="add_shards",
    )(partials, residual.reshape(rows, model_width))
    all_mixed = lax.all_to_all(mixed, "tp", 0, 0)
    next_qkv, new_residual = pl.pallas_call(
        project_kernel,
        out_shape=(
            jax.ShapeDtypeStruct((step_count, 3, row_count, lane_count), jnp.bfloat16),
            jax.ShapeDtypeStruct((rows, model_width), jnp.bfloat16),
        ),
        in_specs=[VMEM_SPEC] * 3,
        out_specs=(VMEM_SPEC, VMEM_SPEC),
        compiler_params=KERNEL_PARAMS,
        name="project",
    )(
        all_mixed,
        norm_gain.reshape(model_width // lane_count, lane_count),
        qkv_weight.transpose(1, 0, 2),
    )
    return (
        next_qkv.transpose(0, 2, 1, 3),
        new_residual.reshape(step_count, row_count, model_width),
    )


def solution(mesh):
    placed = (
        P(None, "req", "tp"),
        P(None, "req", None, "tp"),
        P(None, "req", None),
        P("req", None, None, "tp"),
        P("req", None, None, "tp"),
        P("req", None),
        P("req"),
        P(None, "req"),
        P("req"),
        P("req"),
        P("req"),
        P("tp", None),
        P(),
        P(None, None, "tp"),
    )
    return jax.shard_map(
        shards,
        mesh=mesh,
        in_specs=placed,
        out_specs=(P(None, "req", None, "tp"), P(None, "req", None)),
        check_vma=False,
    )
```

```python
import math

import jax
import jax.numpy as jnp
from jax import lax
from jax.experimental import pallas as pl
from jax.experimental.pallas import tpu as pltpu
from jax.sharding import PartitionSpec as P

HEAD_DIM = 64
BEAMS = 8

NEG_FILL = -1e30
NORM_EPS = 1e-05
SCORE_SCALE = 1.0 / math.sqrt(HEAD_DIM)
LANES = 2 * HEAD_DIM
STAT_ROWS = 8
FIRST_CHIP = 21
SHARD_ORDER = (5, 4, 3, 2, 1, 0, 7, 6)
NOTE_ROWS = 16


def slot_of(device, chips):
    return (device // 2 + chips - FIRST_CHIP % chips) % chips


def split_heads(rows):
    lane = lax.broadcasted_iota(jnp.int32, rows.shape, 1)
    zero = jnp.zeros_like(rows)
    return jnp.concatenate(
        [jnp.where(lane < HEAD_DIM, rows, zero), jnp.where(lane >= HEAD_DIM, rows, zero)], axis=0
    )


def join_heads(rows):
    half = rows.shape[0] // 2
    lane = lax.broadcasted_iota(jnp.int32, (half, rows.shape[1]), 1)
    return jnp.where(lane < HEAD_DIM, rows[:half], rows[half:])


def dot_rows(left, right):
    return lax.dot_general(
        left, right, (((1,), (1,)), ((), ())), preferred_element_type=jnp.float32
    )


def to_value_rows(weights):
    return pltpu.roll(weights, 1, axis=1).astype(jnp.bfloat16)


def prompt_kernel(asked_ref, slots_ref, out_ref):
    core = lax.axis_index("req") % 2
    rows = asked_ref.shape[1]
    tokens = slots_ref.shape[1] - NOTE_ROWS
    lane = lax.broadcasted_iota(jnp.int32, (NOTE_ROWS, LANES), 1)
    row = lax.broadcasted_iota(jnp.int32, (NOTE_ROWS, LANES), 0)
    for slot in range(2):
        note = slots_ref[slot, tokens:].astype(jnp.float32)

        def number(index):
            here = jnp.logical_and(row == 0, lane == index)
            return jnp.sum(jnp.where(here, note, 0.0)).astype(jnp.int32)

        owner = number(0)
        live = number(1) * 16 + number(2)

        @pl.when(owner % 2 == core)
        def _():
            place = slot_of(owner, asked_ref.shape[0])
            out_ref[place] = prompt_packet(asked_ref[place], slots_ref[slot, :tokens], live, rows)


def prompt_packet(query_rows, cache, live, rows):
    queries = split_heads(query_rows)
    scores = dot_rows(queries, cache) * SCORE_SCALE
    column = lax.broadcasted_iota(jnp.int32, scores.shape, 1)
    valid = jnp.logical_and(column % 2 == 0, column < 2 * live)
    scores = jnp.where(valid, scores, NEG_FILL)
    top = jnp.max(scores, axis=1, keepdims=True)
    weights = jnp.exp(scores - top).astype(jnp.bfloat16).astype(jnp.float32)
    total = jnp.sum(weights, axis=1, keepdims=True)
    numer = jnp.dot(to_value_rows(weights), cache, preferred_element_type=jnp.float32)
    mean = join_heads(numer / total).astype(jnp.bfloat16)
    level = top + jnp.log(total)
    high = level.astype(jnp.bfloat16).astype(jnp.float32)
    rest = level - high
    middle = rest.astype(jnp.bfloat16).astype(jnp.float32)
    low = rest - middle
    wide = (2 * rows, LANES)
    lane = lax.broadcasted_iota(jnp.int32, wide, 1)
    row = lax.broadcasted_iota(jnp.int32, wide, 0)
    on_row = lane % HEAD_DIM == row
    first = jnp.sum(
        jnp.where(on_row, jnp.where(lane < HEAD_DIM, high, middle), 0.0), axis=0, keepdims=True
    )
    second = jnp.sum(jnp.where(on_row, low, 0.0), axis=0, keepdims=True)
    stat_row = lax.broadcasted_iota(jnp.int32, (STAT_ROWS, LANES), 0)
    stats = jnp.where(stat_row == 0, first, jnp.where(stat_row == 1, second, 0.0))
    return jnp.concatenate([mean.astype(jnp.float32), stats], axis=0).astype(jnp.bfloat16)


def home_kernel(
    owned_ref,
    live_ref,
    place_ref,
    table_ref,
    length_ref,
    parent_ref,
    query_ref,
    home_ref,
    fresh_ref,
    prompt_ref,
    mean_ref,
    level_ref,
    slot_ref,
    root_ref,
    line_ref,
):
    tokens = prompt_ref.shape[0]
    note_lane = lax.broadcasted_iota(jnp.int32, (NOTE_ROWS, LANES), 1)
    live = live_ref[0]
    note = jnp.where(
        note_lane == 0, owned_ref[0], jnp.where(note_lane == 1, live // 16, live % 16)
    )
    slot_ref[:tokens] = prompt_ref[...]
    slot_ref[tokens:] = note.astype(jnp.float32).astype(jnp.bfloat16)
    step_count = parent_ref.shape[0]
    block_count = table_ref.shape[0]
    rows = query_ref.shape[0]
    block_tokens = home_ref.shape[0] // (2 * block_count)
    unit = (BEAMS, LANES)
    beam_row = lax.broadcasted_iota(jnp.int32, unit, 0)
    lane = lax.broadcasted_iota(jnp.int32, unit, 1)
    is_key = lane % 2 == 0
    half_lane = lane // 2

    def column_of(values):
        built = jnp.full(unit, values[0], jnp.int32)
        for beam in range(1, BEAMS):
            built = jnp.where(beam_row == beam, values[beam], built)
        return built

    counts = []
    fresh_masks = []
    for step in range(step_count):
        roots = []
        for beam in range(BEAMS):
            parent = parent_ref[step, beam]
            root = parent if step == 0 else root_ref[step - 1, parent]
            root_ref[step, beam] = root
            roots.append(root)
            line_ref[step * step_count + step, beam] = beam
            for source in range(step):
                line_ref[step * step_count + source, beam] = line_ref[
                    (step - 1) * step_count + source, parent
                ]
        length = column_of([length_ref[root] for root in roots])
        entries = [
            column_of([table_ref[entry, root] for root in roots]) for entry in range(block_count)
        ]
        pieces = []
        for block in range(block_count):
            limits = [
                jnp.where(entries[entry] == block, length - entry * block_tokens, 0)
                for entry in range(block_count)
            ]
            for part in range(2 * block_tokens // LANES):
                offset = half_lane + part * (LANES // 2)
                count = jnp.zeros(unit, jnp.float32)
                for limit in limits:
                    count = count + jnp.where(offset < limit, 1.0, 0.0)
                pieces.append(jnp.where(is_key, count, 0.0))
        counts.append(jnp.concatenate(pieces, axis=1))
        seen = jnp.zeros(unit, jnp.float32)
        for source in range(step + 1):
            if source == step:
                target = beam_row + source * BEAMS
            else:
                target = (
                    column_of([line_ref[step * step_count + source, beam] for beam in range(BEAMS)])
                    + source * BEAMS
                )
            seen = jnp.where(half_lane == target, 1.0, seen)
        fresh_masks.append(jnp.where(is_key, seen, 0.0))
    count = jnp.concatenate(counts * 2, axis=0)
    fresh_mask = jnp.concatenate(fresh_masks * 2, axis=0)

    queries = split_heads(query_ref[...])
    home = home_ref[...]
    fresh = fresh_ref[...]
    fresh = jnp.concatenate(
        [fresh, jnp.zeros((LANES - fresh.shape[0], LANES), fresh.dtype)], axis=0
    )
    scores = jnp.where(count > 0.0, dot_rows(queries, home) * SCORE_SCALE, NEG_FILL)
    fresh_scores = jnp.where(fresh_mask > 0.0, dot_rows(queries, fresh) * SCORE_SCALE, NEG_FILL)
    top = jnp.maximum(
        jnp.max(scores, axis=1, keepdims=True), jnp.max(fresh_scores, axis=1, keepdims=True)
    )
    weights = jnp.exp(scores - top).astype(jnp.bfloat16).astype(jnp.float32) * count
    weights = weights.astype(jnp.bfloat16).astype(jnp.float32)
    fresh_weights = jnp.exp(fresh_scores - top).astype(jnp.bfloat16).astype(jnp.float32)
    total = jnp.sum(weights, axis=1, keepdims=True) + jnp.sum(fresh_weights, axis=1, keepdims=True)
    numer = jnp.dot(to_value_rows(weights), home, preferred_element_type=jnp.float32)
    numer = numer + jnp.dot(
        to_value_rows(fresh_weights), fresh, preferred_element_type=jnp.float32
    )

    mean_ref[...] = join_heads(numer / total)
    level = jnp.broadcast_to(top + jnp.log(total), numer.shape)
    level_ref[:rows] = join_heads(level)
    level_ref[rows:] = jnp.full((BEAMS, LANES), place_ref[0]).astype(jnp.float32)


def combine_kernel(mean_ref, level_ref, result_ref, weight_ref, out_ref):
    rows = mean_ref.shape[0]
    place = jnp.max(level_ref[rows:]).astype(jnp.int32)
    packet = result_ref[slot_of(place, result_ref.shape[0])].astype(jnp.float32)
    wide = (2 * rows, LANES)
    lane = lax.broadcasted_iota(jnp.int32, wide, 1)
    row = lax.broadcasted_iota(jnp.int32, wide, 0)
    on_row = lane % HEAD_DIM == row
    terms = jnp.broadcast_to(packet[rows : rows + 1], wide) + jnp.where(
        lane < HEAD_DIM, jnp.broadcast_to(packet[rows + 1 : rows + 2], wide), 0.0
    )
    prompt_level = jnp.sum(jnp.where(on_row, terms, 0.0), axis=1, keepdims=True)
    prompt_level = join_heads(jnp.broadcast_to(prompt_level, wide))
    level = level_ref[:rows]
    joint_top = jnp.maximum(level, prompt_level)
    home_factor = jnp.exp(level - joint_top)
    prompt_factor = jnp.exp(prompt_level - joint_top)
    attended = (mean_ref[...] * home_factor + packet[:rows] * prompt_factor) / (
        home_factor + prompt_factor
    )
    partial = jnp.dot(
        attended.astype(jnp.bfloat16), weight_ref[...], preferred_element_type=jnp.float32
    )
    width = out_ref.shape[2]
    for index, shard in enumerate(SHARD_ORDER):
        out_ref[index] = partial[:, shard * width : (shard + 1) * width].astype(out_ref.dtype)


def sum_kernel(partial_ref, residual_ref, out_ref):
    width = partial_ref.shape[2]
    first = pl.multiple_of(lax.axis_index("tp") * width, width)
    mixed = residual_ref[:, pl.ds(first, width)].astype(jnp.float32)
    for index in range(partial_ref.shape[0]):
        mixed = mixed + partial_ref[index].astype(jnp.float32)
    mixed = mixed.astype(jnp.bfloat16)
    for index in range(out_ref.shape[0]):
        out_ref[index] = mixed


def project_kernel(mixed_ref, gain_ref, qkv_weight_ref, qkv_ref, residual_out_ref):
    shards_held = range(mixed_ref.shape[0])
    rounded = jnp.concatenate([mixed_ref[SHARD_ORDER.index(shard)] for shard in shards_held], axis=1)
    residual_out_ref[...] = rounded
    mixed = rounded.astype(jnp.float32)
    mean_square = jnp.mean(mixed * mixed, axis=1, keepdims=True)
    gain_rows = gain_ref[...].astype(jnp.float32)
    gain = jnp.concatenate(
        [gain_rows[index : index + 1] for index in range(gain_rows.shape[0])], axis=1
    )
    normed = (mixed * lax.rsqrt(mean_square + NORM_EPS) * gain).astype(jnp.bfloat16)
    for kind in range(qkv_weight_ref.shape[0]):
        projected = jnp.dot(
            normed, qkv_weight_ref[kind], preferred_element_type=jnp.float32
        ).astype(jnp.bfloat16)
        for step in range(qkv_ref.shape[0]):
            qkv_ref[step, kind] = projected[step * BEAMS : (step + 1) * BEAMS]


VMEM_SPEC = pl.BlockSpec(memory_space=pltpu.VMEM)
SMEM_SPEC = pl.BlockSpec(memory_space=pltpu.SMEM)
KERNEL_PARAMS = pltpu.CompilerParams(vmem_limit_bytes=20 * 1024 * 1024)


def shards(
    queries,
    new_kv,
    residual,
    home_cache,
    prompt_cache,
    home_table,
    home_len,
    parents,
    prompt_place,
    owned_request,
    prompt_len,
    out_weight,
    norm_gain,
    qkv_weight,
):
    step_count, row_count, lane_count = queries.shape
    model_width = residual.shape[-1]
    rows = step_count * row_count
    req_size = lax.axis_size("req")
    tp_size = lax.axis_size("tp")
    chips = req_size // 2
    order = [(position + FIRST_CHIP) % chips for position in range(chips)]
    same_core = [[2 * chip + core for chip in order] for core in range(2)]
    shard_groups = [list(SHARD_ORDER)]
    same_chip = [[2 * chip, 2 * chip + 1] for chip in range(chips)]

    def route(slots):
        return lax.all_to_all(slots, "req", 0, 0, axis_index_groups=same_core)

    query_rows = queries.reshape(rows, lane_count)
    asked = route(jnp.broadcast_to(query_rows[None], (chips, rows, lane_count)))

    home_rows = home_cache.reshape(-1, lane_count)
    fresh_rows = new_kv.reshape(-1, lane_count)
    prompt_rows = prompt_cache.reshape(-1, lane_count)
    slot_rows = prompt_rows.shape[0] + NOTE_ROWS
    home_mean, home_level, own_slot = pl.pallas_call(
        home_kernel,
        out_shape=(
            jax.ShapeDtypeStruct((rows, lane_count), jnp.float32),
            jax.ShapeDtypeStruct((rows + BEAMS, lane_count), jnp.float32),
            jax.ShapeDtypeStruct((slot_rows, lane_count), jnp.bfloat16),
        ),
        in_specs=[SMEM_SPEC] * 6 + [VMEM_SPEC] * 4,
        out_specs=(VMEM_SPEC, VMEM_SPEC, VMEM_SPEC),
        scratch_shapes=[
            pltpu.SMEM((step_count, BEAMS), jnp.int32),
            pltpu.SMEM((step_count * step_count, BEAMS), jnp.int32),
        ],
        name="home_attention",
    )(
        owned_request,
        prompt_len,
        prompt_place,
        home_table.T,
        home_len,
        parents,
        query_rows,
        home_rows,
        fresh_rows,
        prompt_rows,
    )
    both_slots = lax.all_gather(own_slot, "req", axis_index_groups=same_chip)

    packet_rows = rows + STAT_ROWS
    results = pl.pallas_call(
        prompt_kernel,
        out_shape=pltpu.VMEM((chips, packet_rows, lane_count), jnp.bfloat16),
        in_specs=[VMEM_SPEC] * 2,
        out_specs=VMEM_SPEC,
        compiler_params=KERNEL_PARAMS,
        name="prompt_attention",
    )(asked, both_slots)
    returned = route(results)

    width = model_width // tp_size
    partial = pl.pallas_call(
        combine_kernel,
        out_shape=jax.ShapeDtypeStruct((tp_size, rows, width), jnp.bfloat16),
        in_specs=[VMEM_SPEC] * 4,
        out_specs=VMEM_SPEC,
        compiler_params=KERNEL_PARAMS,
        name="combine",
    )(home_mean, home_level, returned, out_weight)
    partials = lax.all_to_all(partial, "tp", 0, 0, axis_index_groups=shard_groups)
    mixed = pl.pallas_call(
        sum_kernel,
        out_shape=jax.ShapeDtypeStruct((tp_size, rows, width), jnp.bfloat16),
        in_specs=[VMEM_SPEC, VMEM_SPEC],
        out_specs=VMEM_SPEC,
        compiler_params=KERNEL_PARAMS,
        name="add_shards",
    )(partials, residual.reshape(rows, model_width))
    all_mixed = lax.all_to_all(mixed, "tp", 0, 0, axis_index_groups=shard_groups)
    next_qkv, new_residual = pl.pallas_call(
        project_kernel,
        out_shape=(
            jax.ShapeDtypeStruct((step_count, 3, row_count, lane_count), jnp.bfloat16),
            jax.ShapeDtypeStruct((rows, model_width), jnp.bfloat16),
        ),
        in_specs=[VMEM_SPEC] * 3,
        out_specs=(VMEM_SPEC, VMEM_SPEC),
        compiler_params=KERNEL_PARAMS,
        name="project",
    )(
        all_mixed,
        norm_gain.reshape(model_width // lane_count, lane_count),
        qkv_weight.transpose(1, 0, 2),
    )
    return (
        next_qkv.transpose(0, 2, 1, 3),
        new_residual.reshape(step_count, row_count, model_width),
    )


def solution(mesh):
    placed = (
        P(None, "req", "tp"),
        P(None, "req", None, "tp"),
        P(None, "req", None),
        P("req", None, None, "tp"),
        P("req", None, None, "tp"),
        P("req", None),
        P("req"),
        P(None, "req"),
        P("req"),
        P("req"),
        P("req"),
        P("tp", None),
        P(),
        P(None, None, "tp"),
    )
    return jax.shard_map(
        shards,
        mesh=mesh,
        in_specs=placed,
        out_specs=(P(None, "req", None, "tp"), P(None, "req", None)),
        check_vma=False,
    )
```

```python
import math

import jax
import jax.numpy as jnp
from jax import lax
from jax.experimental import pallas as pl
from jax.experimental.pallas import tpu as pltpu
from jax.sharding import PartitionSpec as P

HEAD_DIM = 64
BEAMS = 8

NEG_FILL = -1e30
NORM_EPS = 1e-05
SCORE_SCALE = 1.0 / math.sqrt(HEAD_DIM)
LANES = 2 * HEAD_DIM
STAT_ROWS = 2
FIRST_CHIP = 21
SHARD_ORDER = (5, 4, 3, 2, 1, 0, 7, 6)
NOTE_ROWS = 16


def slot_of(device, chips):
    return (device // 2 + chips - FIRST_CHIP % chips) % chips


def split_heads(rows):
    lane = lax.broadcasted_iota(jnp.int32, rows.shape, 1)
    zero = jnp.zeros_like(rows)
    return jnp.concatenate(
        [jnp.where(lane < HEAD_DIM, rows, zero), jnp.where(lane >= HEAD_DIM, rows, zero)], axis=0
    )


def join_heads(rows):
    half = rows.shape[0] // 2
    lane = lax.broadcasted_iota(jnp.int32, (half, rows.shape[1]), 1)
    return jnp.where(lane < HEAD_DIM, rows[:half], rows[half:])


def dot_rows(left, right):
    return lax.dot_general(
        left, right, (((1,), (1,)), ((), ())), preferred_element_type=jnp.float32
    )


def to_value_rows(weights):
    return pltpu.roll(weights, 1, axis=1).astype(jnp.bfloat16)


def prompt_kernel(asked_ref, slots_ref, out_ref):
    core = lax.axis_index("req") % 2
    rows = asked_ref.shape[1]
    tokens = slots_ref.shape[1] - NOTE_ROWS
    lane = lax.broadcasted_iota(jnp.int32, (NOTE_ROWS, LANES), 1)
    row = lax.broadcasted_iota(jnp.int32, (NOTE_ROWS, LANES), 0)
    for slot in range(2):
        note = slots_ref[slot, tokens:].astype(jnp.float32)

        def number(index):
            here = jnp.logical_and(row == 0, lane == index)
            return jnp.sum(jnp.where(here, note, 0.0)).astype(jnp.int32)

        owner = number(0)
        live = number(1) * 16 + number(2)

        @pl.when(owner % 2 == core)
        def _():
            place = slot_of(owner, asked_ref.shape[0])
            out_ref[place] = prompt_packet(asked_ref[place], slots_ref[slot, :tokens], live, rows)


def prompt_packet(query_rows, cache, live, rows):
    queries = split_heads(query_rows)
    scores = dot_rows(queries, cache) * SCORE_SCALE
    column = lax.broadcasted_iota(jnp.int32, scores.shape, 1)
    valid = jnp.logical_and(column % 2 == 0, column < 2 * live)
    scores = jnp.where(valid, scores, NEG_FILL)
    top = jnp.max(scores, axis=1, keepdims=True)
    weights = jnp.exp(scores - top).astype(jnp.bfloat16).astype(jnp.float32)
    total = jnp.sum(weights, axis=1, keepdims=True)
    numer = jnp.dot(to_value_rows(weights), cache, preferred_element_type=jnp.float32)
    mean = join_heads(numer / total).astype(jnp.bfloat16)
    level = top + jnp.log(total)
    high = level.astype(jnp.bfloat16).astype(jnp.float32)
    rest = level - high
    middle = rest.astype(jnp.bfloat16).astype(jnp.float32)
    low = rest - middle
    wide = (2 * rows, LANES)
    lane = lax.broadcasted_iota(jnp.int32, wide, 1)
    row = lax.broadcasted_iota(jnp.int32, wide, 0)
    on_row = lane % HEAD_DIM == row
    first = jnp.sum(
        jnp.where(on_row, jnp.where(lane < HEAD_DIM, high, middle), 0.0), axis=0, keepdims=True
    )
    second = jnp.sum(jnp.where(on_row, low, 0.0), axis=0, keepdims=True)
    mean = mean.astype(jnp.float32)
    pieces = [mean[index : index + 2] for index in range(0, rows, 2)]
    pieces.append(jnp.concatenate([first, second], axis=0))
    return jnp.concatenate(pieces, axis=1).astype(jnp.bfloat16)


def home_kernel(
    owned_ref,
    live_ref,
    place_ref,
    table_ref,
    length_ref,
    parent_ref,
    query_ref,
    home_ref,
    fresh_ref,
    prompt_ref,
    mean_ref,
    level_ref,
    slot_ref,
    root_ref,
    line_ref,
):
    tokens = prompt_ref.shape[0]
    note_lane = lax.broadcasted_iota(jnp.int32, (NOTE_ROWS, LANES), 1)
    live = live_ref[0]
    note = jnp.where(
        note_lane == 0, owned_ref[0], jnp.where(note_lane == 1, live // 16, live % 16)
    )
    slot_ref[:tokens] = prompt_ref[...]
    slot_ref[tokens:] = note.astype(jnp.float32).astype(jnp.bfloat16)
    step_count = parent_ref.shape[0]
    block_count = table_ref.shape[0]
    rows = query_ref.shape[0]
    block_tokens = home_ref.shape[0] // (2 * block_count)
    unit = (BEAMS, LANES)
    beam_row = lax.broadcasted_iota(jnp.int32, unit, 0)
    lane = lax.broadcasted_iota(jnp.int32, unit, 1)
    is_key = lane % 2 == 0
    half_lane = lane // 2

    def column_of(values):
        built = jnp.full(unit, values[0], jnp.int32)
        for beam in range(1, BEAMS):
            built = jnp.where(beam_row == beam, values[beam], built)
        return built

    counts = []
    fresh_masks = []
    for step in range(step_count):
        roots = []
        for beam in range(BEAMS):
            parent = parent_ref[step, beam]
            root = parent if step == 0 else root_ref[step - 1, parent]
            root_ref[step, beam] = root
            roots.append(root)
            line_ref[step * step_count + step, beam] = beam
            for source in range(step):
                line_ref[step * step_count + source, beam] = line_ref[
                    (step - 1) * step_count + source, parent
                ]
        length = column_of([length_ref[root] for root in roots])
        entries = [
            column_of([table_ref[entry, root] for root in roots]) for entry in range(block_count)
        ]
        pieces = []
        for block in range(block_count):
            limits = [
                jnp.where(entries[entry] == block, length - entry * block_tokens, 0)
                for entry in range(block_count)
            ]
            for part in range(2 * block_tokens // LANES):
                offset = half_lane + part * (LANES // 2)
                count = jnp.zeros(unit, jnp.float32)
                for limit in limits:
                    count = count + jnp.where(offset < limit, 1.0, 0.0)
                pieces.append(jnp.where(is_key, count, 0.0))
        counts.append(jnp.concatenate(pieces, axis=1))
        seen = jnp.zeros(unit, jnp.float32)
        for source in range(step + 1):
            if source == step:
                target = beam_row + source * BEAMS
            else:
                target = (
                    column_of([line_ref[step * step_count + source, beam] for beam in range(BEAMS)])
                    + source * BEAMS
                )
            seen = jnp.where(half_lane == target, 1.0, seen)
        fresh_masks.append(jnp.where(is_key, seen, 0.0))
    count = jnp.concatenate(counts * 2, axis=0)
    fresh_mask = jnp.concatenate(fresh_masks * 2, axis=0)

    queries = split_heads(query_ref[...])
    home = home_ref[...]
    fresh = fresh_ref[...]
    fresh = jnp.concatenate(
        [fresh, jnp.zeros((LANES - fresh.shape[0], LANES), fresh.dtype)], axis=0
    )
    scores = jnp.where(count > 0.0, dot_rows(queries, home) * SCORE_SCALE, NEG_FILL)
    fresh_scores = jnp.where(fresh_mask > 0.0, dot_rows(queries, fresh) * SCORE_SCALE, NEG_FILL)
    top = jnp.maximum(
        jnp.max(scores, axis=1, keepdims=True), jnp.max(fresh_scores, axis=1, keepdims=True)
    )
    weights = jnp.exp(scores - top).astype(jnp.bfloat16).astype(jnp.float32) * count
    weights = weights.astype(jnp.bfloat16).astype(jnp.float32)
    fresh_weights = jnp.exp(fresh_scores - top).astype(jnp.bfloat16).astype(jnp.float32)
    total = jnp.sum(weights, axis=1, keepdims=True) + jnp.sum(fresh_weights, axis=1, keepdims=True)
    numer = jnp.dot(to_value_rows(weights), home, preferred_element_type=jnp.float32)
    numer = numer + jnp.dot(
        to_value_rows(fresh_weights), fresh, preferred_element_type=jnp.float32
    )

    mean_ref[...] = join_heads(numer / total)
    level = jnp.broadcast_to(top + jnp.log(total), numer.shape)
    level_ref[:rows] = join_heads(level)
    level_ref[rows:] = jnp.full((BEAMS, LANES), place_ref[0]).astype(jnp.float32)


def combine_kernel(mean_ref, level_ref, result_ref, weight_ref, out_ref):
    rows = mean_ref.shape[0]
    place = jnp.max(level_ref[rows:]).astype(jnp.int32)
    packet = result_ref[slot_of(place, result_ref.shape[0])].astype(jnp.float32)
    pieces = [packet[:, index : index + LANES] for index in range(0, packet.shape[1], LANES)]
    packet = jnp.concatenate(pieces, axis=0)
    wide = (2 * rows, LANES)
    lane = lax.broadcasted_iota(jnp.int32, wide, 1)
    row = lax.broadcasted_iota(jnp.int32, wide, 0)
    on_row = lane % HEAD_DIM == row
    terms = jnp.broadcast_to(packet[rows : rows + 1], wide) + jnp.where(
        lane < HEAD_DIM, jnp.broadcast_to(packet[rows + 1 : rows + 2], wide), 0.0
    )
    prompt_level = jnp.sum(jnp.where(on_row, terms, 0.0), axis=1, keepdims=True)
    prompt_level = join_heads(jnp.broadcast_to(prompt_level, wide))
    level = level_ref[:rows]
    joint_top = jnp.maximum(level, prompt_level)
    home_factor = jnp.exp(level - joint_top)
    prompt_factor = jnp.exp(prompt_level - joint_top)
    attended = (mean_ref[...] * home_factor + packet[:rows] * prompt_factor) / (
        home_factor + prompt_factor
    )
    partial = jnp.dot(
        attended.astype(jnp.bfloat16), weight_ref[...], preferred_element_type=jnp.float32
    )
    width = out_ref.shape[2]
    for index, shard in enumerate(SHARD_ORDER):
        out_ref[index] = partial[:, shard * width : (shard + 1) * width].astype(out_ref.dtype)


def sum_kernel(partial_ref, residual_ref, out_ref):
    width = partial_ref.shape[2]
    first = pl.multiple_of(lax.axis_index("tp") * width, width)
    mixed = residual_ref[:, pl.ds(first, width)].astype(jnp.float32)
    for index in range(partial_ref.shape[0]):
        mixed = mixed + partial_ref[index].astype(jnp.float32)
    mixed = mixed.astype(jnp.bfloat16)
    for index in range(out_ref.shape[0]):
        out_ref[index] = mixed


def project_kernel(mixed_ref, gain_ref, qkv_weight_ref, qkv_ref, residual_out_ref):
    shards_held = range(mixed_ref.shape[0])
    rounded = jnp.concatenate([mixed_ref[SHARD_ORDER.index(shard)] for shard in shards_held], axis=1)
    residual_out_ref[...] = rounded
    mixed = rounded.astype(jnp.float32)
    mean_square = jnp.mean(mixed * mixed, axis=1, keepdims=True)
    gain_rows = gain_ref[...].astype(jnp.float32)
    gain = jnp.concatenate(
        [gain_rows[index : index + 1] for index in range(gain_rows.shape[0])], axis=1
    )
    normed = (mixed * lax.rsqrt(mean_square + NORM_EPS) * gain).astype(jnp.bfloat16)
    for kind in range(qkv_weight_ref.shape[0]):
        projected = jnp.dot(
            normed, qkv_weight_ref[kind], preferred_element_type=jnp.float32
        ).astype(jnp.bfloat16)
        for step in range(qkv_ref.shape[0]):
            qkv_ref[step, kind] = projected[step * BEAMS : (step + 1) * BEAMS]


VMEM_SPEC = pl.BlockSpec(memory_space=pltpu.VMEM)
SMEM_SPEC = pl.BlockSpec(memory_space=pltpu.SMEM)
KERNEL_PARAMS = pltpu.CompilerParams(vmem_limit_bytes=20 * 1024 * 1024)


def shards(
    queries,
    new_kv,
    residual,
    home_cache,
    prompt_cache,
    home_table,
    home_len,
    parents,
    prompt_place,
    owned_request,
    prompt_len,
    out_weight,
    norm_gain,
    qkv_weight,
):
    step_count, row_count, lane_count = queries.shape
    model_width = residual.shape[-1]
    rows = step_count * row_count
    req_size = lax.axis_size("req")
    tp_size = lax.axis_size("tp")
    chips = req_size // 2
    order = [(position + FIRST_CHIP) % chips for position in range(chips)]
    same_core = [[2 * chip + core for chip in order] for core in range(2)]
    shard_groups = [list(SHARD_ORDER)]
    same_chip = [[2 * chip, 2 * chip + 1] for chip in range(chips)]

    def route(slots):
        return lax.all_to_all(slots, "req", 0, 0, axis_index_groups=same_core)

    query_rows = queries.reshape(rows, lane_count)
    asked = route(jnp.broadcast_to(query_rows[None], (chips, rows, lane_count)))

    home_rows = home_cache.reshape(-1, lane_count)
    fresh_rows = new_kv.reshape(-1, lane_count)
    prompt_rows = prompt_cache.reshape(-1, lane_count)
    slot_rows = prompt_rows.shape[0] + NOTE_ROWS
    home_mean, home_level, own_slot = pl.pallas_call(
        home_kernel,
        out_shape=(
            jax.ShapeDtypeStruct((rows, lane_count), jnp.float32),
            jax.ShapeDtypeStruct((rows + BEAMS, lane_count), jnp.float32),
            jax.ShapeDtypeStruct((slot_rows, lane_count), jnp.bfloat16),
        ),
        in_specs=[SMEM_SPEC] * 6 + [VMEM_SPEC] * 4,
        out_specs=(VMEM_SPEC, VMEM_SPEC, VMEM_SPEC),
        scratch_shapes=[
            pltpu.SMEM((step_count, BEAMS), jnp.int32),
            pltpu.SMEM((step_count * step_count, BEAMS), jnp.int32),
        ],
        name="home_attention",
    )(
        owned_request,
        prompt_len,
        prompt_place,
        home_table.T,
        home_len,
        parents,
        query_rows,
        home_rows,
        fresh_rows,
        prompt_rows,
    )
    both_slots = lax.all_gather(own_slot, "req", axis_index_groups=same_chip)

    packet_rows = rows + STAT_ROWS
    results = pl.pallas_call(
        prompt_kernel,
        out_shape=pltpu.VMEM((chips, 2, packet_rows // 2 * lane_count), jnp.bfloat16),
        in_specs=[VMEM_SPEC] * 2,
        out_specs=VMEM_SPEC,
        compiler_params=KERNEL_PARAMS,
        name="prompt_attention",
    )(asked, both_slots)
    returned = route(results)

    width = model_width // tp_size
    partial = pl.pallas_call(
        combine_kernel,
        out_shape=jax.ShapeDtypeStruct((tp_size, rows, width), jnp.bfloat16),
        in_specs=[VMEM_SPEC] * 4,
        out_specs=VMEM_SPEC,
        compiler_params=KERNEL_PARAMS,
        name="combine",
    )(home_mean, home_level, returned, out_weight)
    partials = lax.all_to_all(partial, "tp", 0, 0, axis_index_groups=shard_groups)
    mixed = pl.pallas_call(
        sum_kernel,
        out_shape=jax.ShapeDtypeStruct((tp_size, rows, width), jnp.bfloat16),
        in_specs=[VMEM_SPEC, VMEM_SPEC],
        out_specs=VMEM_SPEC,
        compiler_params=KERNEL_PARAMS,
        name="add_shards",
    )(partials, residual.reshape(rows, model_width))
    all_mixed = lax.all_to_all(mixed, "tp", 0, 0, axis_index_groups=shard_groups)
    next_qkv, new_residual = pl.pallas_call(
        project_kernel,
        out_shape=(
            jax.ShapeDtypeStruct((step_count, 3, row_count, lane_count), jnp.bfloat16),
            jax.ShapeDtypeStruct((rows, model_width), jnp.bfloat16),
        ),
        in_specs=[VMEM_SPEC] * 3,
        out_specs=(VMEM_SPEC, VMEM_SPEC),
        compiler_params=KERNEL_PARAMS,
        name="project",
    )(
        all_mixed,
        norm_gain.reshape(model_width // lane_count, lane_count),
        qkv_weight.transpose(1, 0, 2),
    )
    return (
        next_qkv.transpose(0, 2, 1, 3),
        new_residual.reshape(step_count, row_count, model_width),
    )


def solution(mesh):
    placed = (
        P(None, "req", "tp"),
        P(None, "req", None, "tp"),
        P(None, "req", None),
        P("req", None, None, "tp"),
        P("req", None, None, "tp"),
        P("req", None),
        P("req"),
        P(None, "req"),
        P("req"),
        P("req"),
        P("req"),
        P("tp", None),
        P(),
        P(None, None, "tp"),
    )
    return jax.shard_map(
        shards,
        mesh=mesh,
        in_specs=placed,
        out_specs=(P(None, "req", None, "tp"), P(None, "req", None)),
        check_vma=False,
    )
```

```python
import math

import jax
import jax.numpy as jnp
from jax import lax
from jax.experimental import pallas as pl
from jax.experimental.pallas import tpu as pltpu
from jax.sharding import PartitionSpec as P

HEAD_DIM = 64
BEAMS = 8

NEG_FILL = -1e30
NORM_EPS = 1e-05
SCORE_SCALE = 1.0 / math.sqrt(HEAD_DIM)
LANES = 2 * HEAD_DIM
STAT_ROWS = 2
FIRST_CHIP = 21
SHARD_ORDER = (5, 4, 3, 2, 1, 0, 7, 6)
NOTE_ROWS = 16


def slot_of(device, chips):
    return (device // 2 + chips - FIRST_CHIP % chips) % chips


def split_heads(rows):
    lane = lax.broadcasted_iota(jnp.int32, rows.shape, 1)
    zero = jnp.zeros_like(rows)
    return jnp.concatenate(
        [jnp.where(lane < HEAD_DIM, rows, zero), jnp.where(lane >= HEAD_DIM, rows, zero)], axis=0
    )


def join_heads(rows):
    half = rows.shape[0] // 2
    lane = lax.broadcasted_iota(jnp.int32, (half, rows.shape[1]), 1)
    return jnp.where(lane < HEAD_DIM, rows[:half], rows[half:])


def dot_rows(left, right):
    return lax.dot_general(
        left, right, (((1,), (1,)), ((), ())), preferred_element_type=jnp.float32
    )


def to_value_rows(weights):
    return pltpu.roll(weights, 1, axis=1).astype(jnp.bfloat16)


def prompt_kernel(asked_ref, slots_ref, out_ref):
    core = lax.axis_index("req") % 2
    rows = asked_ref.shape[1]
    tokens = slots_ref.shape[1] - NOTE_ROWS
    lane = lax.broadcasted_iota(jnp.int32, (NOTE_ROWS, LANES), 1)
    row = lax.broadcasted_iota(jnp.int32, (NOTE_ROWS, LANES), 0)
    served = []
    for slot in range(2):
        note = slots_ref[slot, tokens:].astype(jnp.float32)

        def number(index):
            here = jnp.logical_and(row == 0, lane == index)
            return jnp.sum(jnp.where(here, note, 0.0)).astype(jnp.int32)

        owner = number(0)
        live = number(1) * 16 + number(2)

        place = slot_of(owner, asked_ref.shape[0])
        packet = prompt_packet(asked_ref[place], slots_ref[slot, :tokens], live, rows)
        served.append((owner, place, packet))
    for owner, place, packet in served:

        @pl.when(owner % 2 == core)
        def _():
            out_ref[place] = packet


def prompt_packet(query_rows, cache, live, rows):
    queries = split_heads(query_rows)
    scores = dot_rows(queries, cache) * SCORE_SCALE
    column = lax.broadcasted_iota(jnp.int32, scores.shape, 1)
    valid = jnp.logical_and(column % 2 == 0, column < 2 * live)
    scores = jnp.where(valid, scores, NEG_FILL)
    top = jnp.max(scores, axis=1, keepdims=True)
    weights = jnp.exp(scores - top).astype(jnp.bfloat16).astype(jnp.float32)
    total = jnp.sum(weights, axis=1, keepdims=True)
    numer = jnp.dot(to_value_rows(weights), cache, preferred_element_type=jnp.float32)
    mean = join_heads(numer / total).astype(jnp.bfloat16)
    level = top + jnp.log(total)
    high = level.astype(jnp.bfloat16).astype(jnp.float32)
    rest = level - high
    middle = rest.astype(jnp.bfloat16).astype(jnp.float32)
    low = rest - middle
    wide = (2 * rows, LANES)
    lane = lax.broadcasted_iota(jnp.int32, wide, 1)
    row = lax.broadcasted_iota(jnp.int32, wide, 0)
    on_row = lane % HEAD_DIM == row
    first = jnp.sum(
        jnp.where(on_row, jnp.where(lane < HEAD_DIM, high, middle), 0.0), axis=0, keepdims=True
    )
    second = jnp.sum(jnp.where(on_row, low, 0.0), axis=0, keepdims=True)
    mean = mean.astype(jnp.float32)
    pieces = [mean[index : index + 2] for index in range(0, rows, 2)]
    pieces.append(jnp.concatenate([first, second], axis=0))
    return jnp.concatenate(pieces, axis=1).astype(jnp.bfloat16)


def home_kernel(
    owned_ref,
    live_ref,
    place_ref,
    table_ref,
    length_ref,
    parent_ref,
    query_ref,
    home_ref,
    fresh_ref,
    prompt_ref,
    mean_ref,
    level_ref,
    slot_ref,
    root_ref,
    line_ref,
):
    tokens = prompt_ref.shape[0]
    note_lane = lax.broadcasted_iota(jnp.int32, (NOTE_ROWS, LANES), 1)
    live = live_ref[0]
    note = jnp.where(
        note_lane == 0, owned_ref[0], jnp.where(note_lane == 1, live // 16, live % 16)
    )
    slot_ref[:tokens] = prompt_ref[...]
    slot_ref[tokens:] = note.astype(jnp.float32).astype(jnp.bfloat16)
    step_count = parent_ref.shape[0]
    block_count = table_ref.shape[0]
    rows = query_ref.shape[0]
    block_tokens = home_ref.shape[0] // (2 * block_count)
    unit = (BEAMS, LANES)
    beam_row = lax.broadcasted_iota(jnp.int32, unit, 0)
    lane = lax.broadcasted_iota(jnp.int32, unit, 1)
    is_key = lane % 2 == 0
    half_lane = lane // 2

    def column_of(values):
        built = jnp.full(unit, values[0], jnp.int32)
        for beam in range(1, BEAMS):
            built = jnp.where(beam_row == beam, values[beam], built)
        return built

    counts = []
    fresh_masks = []
    for step in range(step_count):
        roots = []
        for beam in range(BEAMS):
            parent = parent_ref[step, beam]
            root = parent if step == 0 else root_ref[step - 1, parent]
            root_ref[step, beam] = root
            roots.append(root)
            line_ref[step * step_count + step, beam] = beam
            for source in range(step):
                line_ref[step * step_count + source, beam] = line_ref[
                    (step - 1) * step_count + source, parent
                ]
        length = column_of([length_ref[root] for root in roots])
        entries = [
            column_of([table_ref[entry, root] for root in roots]) for entry in range(block_count)
        ]
        pieces = []
        for block in range(block_count):
            limits = [
                jnp.where(entries[entry] == block, length - entry * block_tokens, 0)
                for entry in range(block_count)
            ]
            for part in range(2 * block_tokens // LANES):
                offset = half_lane + part * (LANES // 2)
                count = jnp.zeros(unit, jnp.float32)
                for limit in limits:
                    count = count + jnp.where(offset < limit, 1.0, 0.0)
                pieces.append(jnp.where(is_key, count, 0.0))
        counts.append(jnp.concatenate(pieces, axis=1))
        seen = jnp.zeros(unit, jnp.float32)
        for source in range(step + 1):
            if source == step:
                target = beam_row + source * BEAMS
            else:
                target = (
                    column_of([line_ref[step * step_count + source, beam] for beam in range(BEAMS)])
                    + source * BEAMS
                )
            seen = jnp.where(half_lane == target, 1.0, seen)
        fresh_masks.append(jnp.where(is_key, seen, 0.0))
    count = jnp.concatenate(counts * 2, axis=0)
    fresh_mask = jnp.concatenate(fresh_masks * 2, axis=0)

    queries = split_heads(query_ref[...])
    home = home_ref[...]
    fresh = fresh_ref[...]
    fresh = jnp.concatenate(
        [fresh, jnp.zeros((LANES - fresh.shape[0], LANES), fresh.dtype)], axis=0
    )
    scores = jnp.where(count > 0.0, dot_rows(queries, home) * SCORE_SCALE, NEG_FILL)
    fresh_scores = jnp.where(fresh_mask > 0.0, dot_rows(queries, fresh) * SCORE_SCALE, NEG_FILL)
    top = jnp.maximum(
        jnp.max(scores, axis=1, keepdims=True), jnp.max(fresh_scores, axis=1, keepdims=True)
    )
    weights = jnp.exp(scores - top).astype(jnp.bfloat16).astype(jnp.float32) * count
    weights = weights.astype(jnp.bfloat16).astype(jnp.float32)
    fresh_weights = jnp.exp(fresh_scores - top).astype(jnp.bfloat16).astype(jnp.float32)
    total = jnp.sum(weights, axis=1, keepdims=True) + jnp.sum(fresh_weights, axis=1, keepdims=True)
    numer = jnp.dot(to_value_rows(weights), home, preferred_element_type=jnp.float32)
    numer = numer + jnp.dot(
        to_value_rows(fresh_weights), fresh, preferred_element_type=jnp.float32
    )

    mean_ref[...] = join_heads(numer / total)
    level = jnp.broadcast_to(top + jnp.log(total), numer.shape)
    level_ref[:rows] = join_heads(level)
    level_ref[rows:] = jnp.full((BEAMS, LANES), place_ref[0]).astype(jnp.float32)


def combine_kernel(mean_ref, level_ref, result_ref, weight_ref, out_ref):
    rows = mean_ref.shape[0]
    place = jnp.max(level_ref[rows:]).astype(jnp.int32)
    packet = result_ref[slot_of(place, result_ref.shape[0])].astype(jnp.float32)
    pieces = [packet[:, index : index + LANES] for index in range(0, packet.shape[1], LANES)]
    packet = jnp.concatenate(pieces, axis=0)
    wide = (2 * rows, LANES)
    lane = lax.broadcasted_iota(jnp.int32, wide, 1)
    row = lax.broadcasted_iota(jnp.int32, wide, 0)
    on_row = lane % HEAD_DIM == row
    terms = jnp.broadcast_to(packet[rows : rows + 1], wide) + jnp.where(
        lane < HEAD_DIM, jnp.broadcast_to(packet[rows + 1 : rows + 2], wide), 0.0
    )
    prompt_level = jnp.sum(jnp.where(on_row, terms, 0.0), axis=1, keepdims=True)
    prompt_level = join_heads(jnp.broadcast_to(prompt_level, wide))
    level = level_ref[:rows]
    joint_top = jnp.maximum(level, prompt_level)
    home_factor = jnp.exp(level - joint_top)
    prompt_factor = jnp.exp(prompt_level - joint_top)
    attended = (mean_ref[...] * home_factor + packet[:rows] * prompt_factor) / (
        home_factor + prompt_factor
    )
    partial = jnp.dot(
        attended.astype(jnp.bfloat16), weight_ref[...], preferred_element_type=jnp.float32
    )
    width = out_ref.shape[2]
    for index, shard in enumerate(SHARD_ORDER):
        out_ref[index] = partial[:, shard * width : (shard + 1) * width].astype(out_ref.dtype)


def sum_kernel(partial_ref, residual_ref, out_ref):
    width = partial_ref.shape[2]
    first = pl.multiple_of(lax.axis_index("tp") * width, width)
    mixed = residual_ref[:, pl.ds(first, width)].astype(jnp.float32)
    for index in range(partial_ref.shape[0]):
        mixed = mixed + partial_ref[index].astype(jnp.float32)
    mixed = mixed.astype(jnp.bfloat16)
    for index in range(out_ref.shape[0]):
        out_ref[index] = mixed


def project_kernel(mixed_ref, gain_ref, qkv_weight_ref, qkv_ref, residual_out_ref):
    shards_held = range(mixed_ref.shape[0])
    rounded = jnp.concatenate([mixed_ref[SHARD_ORDER.index(shard)] for shard in shards_held], axis=1)
    residual_out_ref[...] = rounded
    mixed = rounded.astype(jnp.float32)
    mean_square = jnp.mean(mixed * mixed, axis=1, keepdims=True)
    gain_rows = gain_ref[...].astype(jnp.float32)
    gain = jnp.concatenate(
        [gain_rows[index : index + 1] for index in range(gain_rows.shape[0])], axis=1
    )
    normed = (mixed * lax.rsqrt(mean_square + NORM_EPS) * gain).astype(jnp.bfloat16)
    for kind in range(qkv_weight_ref.shape[0]):
        projected = jnp.dot(
            normed, qkv_weight_ref[kind], preferred_element_type=jnp.float32
        ).astype(jnp.bfloat16)
        for step in range(qkv_ref.shape[0]):
            qkv_ref[step, kind] = projected[step * BEAMS : (step + 1) * BEAMS]


VMEM_SPEC = pl.BlockSpec(memory_space=pltpu.VMEM)
SMEM_SPEC = pl.BlockSpec(memory_space=pltpu.SMEM)
KERNEL_PARAMS = pltpu.CompilerParams(vmem_limit_bytes=20 * 1024 * 1024)


def shards(
    queries,
    new_kv,
    residual,
    home_cache,
    prompt_cache,
    home_table,
    home_len,
    parents,
    prompt_place,
    owned_request,
    prompt_len,
    out_weight,
    norm_gain,
    qkv_weight,
):
    step_count, row_count, lane_count = queries.shape
    model_width = residual.shape[-1]
    rows = step_count * row_count
    req_size = lax.axis_size("req")
    tp_size = lax.axis_size("tp")
    chips = req_size // 2
    order = [(position + FIRST_CHIP) % chips for position in range(chips)]
    same_core = [[2 * chip + core for chip in order] for core in range(2)]
    shard_groups = [list(SHARD_ORDER)]
    same_chip = [[2 * chip, 2 * chip + 1] for chip in range(chips)]

    def route(slots):
        return lax.all_to_all(slots, "req", 0, 0, axis_index_groups=same_core)

    query_rows = queries.reshape(rows, lane_count)
    asked = route(jnp.broadcast_to(query_rows[None], (chips, rows, lane_count)))

    home_rows = home_cache.reshape(-1, lane_count)
    fresh_rows = new_kv.reshape(-1, lane_count)
    prompt_rows = prompt_cache.reshape(-1, lane_count)
    slot_rows = prompt_rows.shape[0] + NOTE_ROWS
    home_mean, home_level, own_slot = pl.pallas_call(
        home_kernel,
        out_shape=(
            jax.ShapeDtypeStruct((rows, lane_count), jnp.float32),
            jax.ShapeDtypeStruct((rows + BEAMS, lane_count), jnp.float32),
            jax.ShapeDtypeStruct((slot_rows, lane_count), jnp.bfloat16),
        ),
        in_specs=[SMEM_SPEC] * 6 + [VMEM_SPEC] * 4,
        out_specs=(VMEM_SPEC, VMEM_SPEC, VMEM_SPEC),
        scratch_shapes=[
            pltpu.SMEM((step_count, BEAMS), jnp.int32),
            pltpu.SMEM((step_count * step_count, BEAMS), jnp.int32),
        ],
        name="home_attention",
    )(
        owned_request,
        prompt_len,
        prompt_place,
        home_table.T,
        home_len,
        parents,
        query_rows,
        home_rows,
        fresh_rows,
        prompt_rows,
    )
    both_slots = lax.all_gather(own_slot, "req", axis_index_groups=same_chip)

    packet_rows = rows + STAT_ROWS
    results = pl.pallas_call(
        prompt_kernel,
        out_shape=pltpu.VMEM((chips, 2, packet_rows // 2 * lane_count), jnp.bfloat16),
        in_specs=[VMEM_SPEC] * 2,
        out_specs=VMEM_SPEC,
        compiler_params=KERNEL_PARAMS,
        name="prompt_attention",
    )(asked, both_slots)
    returned = route(results)

    width = model_width // tp_size
    partial = pl.pallas_call(
        combine_kernel,
        out_shape=jax.ShapeDtypeStruct((tp_size, rows, width), jnp.bfloat16),
        in_specs=[VMEM_SPEC] * 4,
        out_specs=VMEM_SPEC,
        compiler_params=KERNEL_PARAMS,
        name="combine",
    )(home_mean, home_level, returned, out_weight)
    partials = lax.all_to_all(partial, "tp", 0, 0, axis_index_groups=shard_groups)
    mixed = pl.pallas_call(
        sum_kernel,
        out_shape=jax.ShapeDtypeStruct((tp_size, rows, width), jnp.bfloat16),
        in_specs=[VMEM_SPEC, VMEM_SPEC],
        out_specs=VMEM_SPEC,
        compiler_params=KERNEL_PARAMS,
        name="add_shards",
    )(partials, residual.reshape(rows, model_width))
    all_mixed = lax.all_to_all(mixed, "tp", 0, 0, axis_index_groups=shard_groups)
    next_qkv, new_residual = pl.pallas_call(
        project_kernel,
        out_shape=(
            jax.ShapeDtypeStruct((step_count, 3, row_count, lane_count), jnp.bfloat16),
            jax.ShapeDtypeStruct((rows, model_width), jnp.bfloat16),
        ),
        in_specs=[VMEM_SPEC] * 3,
        out_specs=(VMEM_SPEC, VMEM_SPEC),
        compiler_params=KERNEL_PARAMS,
        name="project",
    )(
        all_mixed,
        norm_gain.reshape(model_width // lane_count, lane_count),
        qkv_weight.transpose(1, 0, 2),
    )
    return (
        next_qkv.transpose(0, 2, 1, 3),
        new_residual.reshape(step_count, row_count, model_width),
    )


def solution(mesh):
    placed = (
        P(None, "req", "tp"),
        P(None, "req", None, "tp"),
        P(None, "req", None),
        P("req", None, None, "tp"),
        P("req", None, None, "tp"),
        P("req", None),
        P("req"),
        P(None, "req"),
        P("req"),
        P("req"),
        P("req"),
        P("tp", None),
        P(),
        P(None, None, "tp"),
    )
    return jax.shard_map(
        shards,
        mesh=mesh,
        in_specs=placed,
        out_specs=(P(None, "req", None, "tp"), P(None, "req", None)),
        check_vma=False,
    )
```
